32 devices in a mesh: cone: 4 (over y, x), con: 8 (over z, core).
Axes of the slice: x: 2, y: 2, z: 4, core: 2. Of those that a mesh axis runs over, the one named last changes fastest.
Arguments:
- vectors: bfloat16 [4, 8192, 1024], P('cone', 'con'), may hold values from -0.1875 to 0.1875
- primal: bfloat16 [4, 1024, 1024], P('cone'), may hold values from -8 to 8, as said below
- dual_inverse: bfloat16 [4, 1024, 1024], P('cone'), may hold values from -8 to 8, as said below
- touches: int32 [4, 8], P('cone'), may hold values from 0 to 1, as said below
Outputs:
- slab: float32 [2048, 8192], P('cone', 'con')
The draws below stay inside these ranges and needn't reach their ends.
Inputs may be any that keep to these rules, and one draw needn't show every extreme that they name: `primal`: symmetric and positive definite in every cone. `dual_inverse`: symmetric and positive definite in every cone. Every constraint block touches at least one cone.
All inputs are finite; a program needn't handle non-finite values.
Results may differ from the reference program's by a relative error of at most 0.00079.
Values may be sent and summed in bfloat16 or wider, within the bound.
No kernel may reach another device: no remote copies, remote signals or barrier semaphores. Data moves between devices by JAX's collectives and lax.ppermute only.
A program may use at most 128 MiB of HBM per device.

```python
import jax
import jax.numpy as jnp
from jax import lax

NC = 1024
CON_DEV = 1024
PANEL = 512
COLUMNS = 8192
CONES = 4
BLOCKS = 8
N_CONE = 4
N_CON = 8


def definite_draw(key, salt_value):
    base_key = jax.random.fold_in(key, salt_value)
    first_key, second_key = jax.random.split(base_key)
    spread = jax.random.normal(first_key, (CONES, NC, NC), jnp.float32)
    diagonal = jax.random.uniform(second_key, (CONES, NC), jnp.float32, 0.5, 1.0)
    gram = jnp.einsum('cik,cjk->cij', spread, spread, precision=lax.Precision.HIGHEST) / NC
    gram = (gram + jnp.swapaxes(gram, 1, 2)) * 0.5
    identity = jnp.eye(NC, dtype=jnp.float32)[None]
    return (gram + diagonal[:, :, None] * identity).astype(jnp.bfloat16)


def draw_vectors(key, part):
    base_key = jax.random.fold_in(key, 53)
    noise_key, common_key = jax.random.split(base_key)
    unit = jnp.float32(NC) ** (-0.5)
    common = jax.random.normal(common_key, (CONES, 1, NC), jnp.float32) * unit
    noise = jax.random.normal(noise_key, (CONES, COLUMNS, NC), jnp.float32) * unit
    mixed = noise + 0.5 * common
    return jnp.clip(mixed, -6.0 * unit, 6.0 * unit).astype(jnp.bfloat16)


def draw_primal(key, part):
    return definite_draw(key, 11)


def draw_dual_inverse(key, part):
    return definite_draw(key, 23)


def draw_touches(key, part):
    base_key = jax.random.fold_in(key, 37)
    level_key, entry_key, home_key = jax.random.split(base_key, 3)
    levels = jax.random.randint(level_key, (CONES, 1), 0, 5)
    threshold = jnp.power(2, levels)
    entries = jax.random.randint(entry_key, (CONES, BLOCKS), 0, 16)
    homes = jax.random.randint(home_key, (1, BLOCKS), 0, CONES)
    cone_ids = jnp.arange(CONES, dtype=jnp.int32)[:, None]
    return ((entries < threshold) | (cone_ids == homes)).astype(jnp.int32)


def setup_inputs(seed: int = 0) -> dict:
    splits = jax.random.split(jax.random.key(seed), 5)
    vectors = draw_vectors(jax.random.fold_in(splits[4], 71), 0)
    primal = draw_primal(jax.random.fold_in(splits[4], 71), 0)
    dual_inverse = draw_dual_inverse(jax.random.fold_in(splits[4], 71), 0)
    touches = draw_touches(jax.random.fold_in(splits[4], 71), 0)
    return {"vectors": vectors, "primal": primal, "dual_inverse": dual_inverse, "touches": touches}


def row_constraints(row_dev):
    positions = jnp.arange(PANEL * N_CONE, dtype=jnp.int32)
    return (positions // row_dev * CON_DEV + positions % row_dev).astype(jnp.int32)

def reference(vectors, primal, dual_inverse, touches):
    row_dev = PANEL * N_CONE // N_CON
    columns_total = CON_DEV * N_CON
    column_ids = jnp.arange(columns_total, dtype=jnp.int32)
    column_block = column_ids // CON_DEV
    keep_flags = touches[:, column_block].astype(vectors.dtype)
    masked = vectors * keep_flags[:, :, None]
    chosen = row_constraints(row_dev)

    def one_cone(running, inputs):
        cone_vectors, primal_block, dual_block = inputs
        row_vectors = cone_vectors[chosen]
        row_primal = jnp.dot(row_vectors.astype(jnp.float32), primal_block.astype(jnp.float32), preferred_element_type=jnp.float32).astype(jnp.bfloat16)
        row_dual = jnp.dot(row_vectors.astype(jnp.float32), dual_block.astype(jnp.float32), preferred_element_type=jnp.float32).astype(jnp.bfloat16)
        gram_primal = jnp.dot(row_primal.astype(jnp.float32), cone_vectors.T.astype(jnp.float32), preferred_element_type=jnp.float32)
        gram_dual = jnp.dot(row_dual.astype(jnp.float32), cone_vectors.T.astype(jnp.float32), preferred_element_type=jnp.float32)
        return (running + gram_primal * gram_dual, None)
    schur_slab, _unused = lax.scan(one_cone, jnp.zeros((PANEL * N_CONE, columns_total), jnp.float32), (masked, primal, dual_inverse))
    panel_block = schur_slab[:PANEL]
    pivot_source = panel_block[:, chosen[:PANEL]]
    pivot_matrix = (pivot_source + pivot_source.T) * 0.5
    lower_factor = jnp.linalg.cholesky(pivot_matrix)
    factor_rows = jax.scipy.linalg.solve_triangular(lower_factor, panel_block, lower=True)
    row_factor = factor_rows[:, chosen]
    updated = schur_slab - jnp.einsum('kr,kc->rc', row_factor, factor_rows, precision=lax.Precision.HIGHEST)
    pivot_column = (column_block < N_CON // N_CONE) & (column_ids % CON_DEV < row_dev)
    remaining = jnp.where(pivot_column[None, :], 0.0, updated)
    return jnp.concatenate([factor_rows, remaining[PANEL:]], axis=0)
```

```python
import jax
import jax.numpy as jnp
from jax import lax
from jax.experimental import pallas as pl
from jax.experimental.pallas import tpu as pltpu
from jax.sharding import PartitionSpec as P

PANEL = 512
HI = lax.Precision.HIGHEST

TILE=128
SUB=8

def factor_tile(a):
    groups=TILE//SUB
    rows=lax.broadcasted_iota(jnp.int32,(SUB,TILE),0)
    lanes=lax.broadcasted_iota(jnp.int32,(SUB,TILE),1)
    left=[a[g*SUB:(g+1)*SUB,:] for g in range(groups)]
    right=[jnp.where(lanes==rows+g*SUB,1.0,0.0).astype(jnp.float32) for g in range(groups)]
    spread=lambda x,j: jnp.broadcast_to(x[:,j:j+1],(SUB,TILE))
    flat=lambda x,i: jnp.broadcast_to(x[i:i+1,:],(SUB,TILE))
    col=[spread(x,0) for x in left]
    pivots=[jnp.ones((SUB,TILE),jnp.float32) for _ in range(groups)]
    for j in range(TILE):
        g0,i0=divmod(j,SUB)
        d=flat(col[g0],i0)
        inv=1.0/d
        pivots[g0]=jnp.where(rows==i0,d,pivots[g0])
        if j==TILE-1: break
        g1,i1=divmod(j+1,SUB)
        nxt=[spread(left[g],j+1) if g>=g1 else None for g in range(groups)]
        c1=flat(col[g1],i1)
        lrow=flat(left[g0],i0); rrow=flat(right[g0],i0)
        new=[None]*groups
        for g in range(g0,groups):
            m=col[g]*inv
            if g==g0: m=jnp.where(rows>i0,m,0.0)
            if g>=g1: new[g]=nxt[g]-m*c1
            left[g]=left[g]-m*lrow
            right[g]=right[g]-m*rrow
        col=new
    return jnp.concatenate([r*lax.rsqrt(p) for r,p in zip(right,pivots)],axis=0)

def inverse_kernel(a_ref,x_ref,work):
    n=a_ref.shape[0]; tiles=n//TILE
    r=lax.broadcasted_iota(jnp.int32,(n,n),0); c=lax.broadcasted_iota(jnp.int32,(n,n),1)
    work[...]=a_ref[...]
    x_ref[...]=jnp.where(r==c,1.0,0.0).astype(jnp.float32)
    def step(p,carry):
        here=pl.ds(pl.multiple_of(p*TILE,TILE),TILE)
        tile=factor_tile(work[here,here])
        upper=jnp.dot(tile,work[here,:],precision=HI,preferred_element_type=jnp.float32)
        solved=jnp.dot(tile,x_ref[here,:],precision=HI,preferred_element_type=jnp.float32)
        x_ref[here,:]=solved
        for q in range(1,tiles):
            @pl.when(q>p)
            def _():
                below=slice(q*TILE,(q+1)*TILE)
                w=upper[:,below]
                ct=(((0,),(0,)),((),()))
                work[below,:]-=lax.dot_general(w,upper,ct,precision=HI,preferred_element_type=jnp.float32)
                x_ref[below,:]-=lax.dot_general(w,solved,ct,precision=HI,preferred_element_type=jnp.float32)
        return carry
    lax.fori_loop(0,tiles,step,0)

def inverse_factor(a):
    n=a.shape[0]
    return pl.pallas_call(inverse_kernel,out_shape=jax.ShapeDtypeStruct((n,n),jnp.float32),
        in_specs=[pl.BlockSpec(memory_space=pltpu.VMEM)],out_specs=pl.BlockSpec(memory_space=pltpu.VMEM),
        scratch_shapes=[pltpu.VMEM((n,n),jnp.float32)],name="inverse_factor")(a)


def broadcast(value, axis, source):
    kept = jnp.where(lax.axis_index(axis) == source, value, 0).astype(value.dtype)
    return lax.psum(kept, axis)


def shards(vectors, primal, dual_inverse, touches):
    con_count = lax.axis_size("con")
    cone_count = lax.axis_size("cone")
    con_place = lax.axis_index("con")
    cone_place = lax.axis_index("cone")
    per_block = vectors.shape[1]
    row_dev = PANEL * cone_count // con_count
    owners = con_count // cone_count
    touched = touches[0]
    own_flag = lax.dynamic_index_in_dim(touched, con_place, 0, keepdims=False)
    own_vectors = vectors[0] * own_flag.astype(jnp.bfloat16)
    primal_block = primal[0]
    dual_block = dual_inverse[0]
    row_vectors = lax.all_gather(own_vectors[:row_dev], "con", axis=0, tiled=True)
    row_primal = jnp.dot(row_vectors, primal_block, preferred_element_type=jnp.float32).astype(
        jnp.bfloat16
    )
    row_dual = jnp.dot(row_vectors, dual_block, preferred_element_type=jnp.float32).astype(
        jnp.bfloat16
    )
    contract = (((1,), (1,)), ((), ()))
    gram_primal = lax.dot_general(
        row_primal, own_vectors, contract, preferred_element_type=jnp.float32
    )
    gram_dual = lax.dot_general(row_dual, own_vectors, contract, preferred_element_type=jnp.float32)
    schur_slab = lax.psum_scatter(gram_primal * gram_dual, "cone", scatter_dimension=0, tiled=True)
    panel_block = broadcast(schur_slab, "cone", 0)
    leading_columns = panel_block[:, :row_dev]
    gathered = lax.all_gather(leading_columns, "con", axis=1, tiled=True)
    pivot_source = gathered[:, :PANEL]
    block_source = lax.dynamic_slice_in_dim(gathered, cone_place * PANEL, PANEL, 1)
    pivot_matrix = (pivot_source + pivot_source.T) * 0.5
    inverse = inverse_factor(pivot_matrix)
    combined = jnp.concatenate([panel_block, block_source], axis=1)
    solved = jnp.dot(inverse, combined, precision=HI)
    factor_rows = solved[:, :per_block]
    row_factor = solved[:, per_block:]
    updated = schur_slab - jnp.einsum(
        "kr,kc->rc", row_factor, factor_rows, precision=lax.Precision.HIGHEST
    )
    local_columns = jnp.arange(per_block, dtype=jnp.int32)
    pivot_column = (con_place < owners) & (local_columns < row_dev)
    remaining = jnp.where(pivot_column[None, :], 0.0, updated)
    return jnp.where(cone_place == 0, factor_rows, remaining)


def solution(mesh):
    in_specs = (
        P("cone", "con", None),
        P("cone", None, None),
        P("cone", None, None),
        P("cone", None),
    )
    out_specs = P("cone", "con")
    return jax.shard_map(shards, mesh=mesh, in_specs=in_specs, out_specs=out_specs, check_vma=False)
```

```python
import functools
import math

import jax
import jax.numpy as jnp
from jax import lax
from jax.experimental import pallas as pl
from jax.experimental.pallas import tpu as pltpu
from jax.sharding import PartitionSpec as P

PANEL = 512
TILE = 128
SUB = 8
STEPS = 128
LEVELS = 32767.0
OCTAVE = math.log(2.0) / STEPS
HI = lax.Precision.HIGHEST
ROWS_T = (((1,), (1,)), ((), ()))
COLS_T = (((0,), (0,)), ((), ()))
F32 = jnp.float32
BF16 = jnp.bfloat16
I16 = jnp.int16


def in_vmem(count):
    return [pl.BlockSpec(memory_space=pltpu.VMEM)] * count


def in_smem():
    return pl.BlockSpec(memory_space=pltpu.SMEM)


def shaped(rows, columns, dtype):
    return jax.ShapeDtypeStruct((rows, columns), dtype)


def encode(value, out_ref, start):
    rows = value.shape[0]
    top = jnp.max(jnp.abs(value), axis=0, keepdims=True)
    level = jnp.ceil(jnp.log(jnp.maximum(top, 1e-37)) * (1.0 / OCTAVE))
    scaled = value * jnp.exp(level * -OCTAVE) * LEVELS
    whole = jnp.round(jnp.clip(scaled, -LEVELS, LEVELS)).astype(jnp.int32)
    out_ref[start : start + rows, :] = whole.astype(I16)
    levels = jnp.broadcast_to(level, (SUB, value.shape[1])).astype(jnp.int32)
    out_ref[start + rows : start + rows + SUB, :] = levels.astype(I16)


def decode(ref, start, rows):
    whole = ref[start : start + rows, :].astype(jnp.int32).astype(F32)
    level = ref[start + rows : start + rows + SUB, :].astype(jnp.int32).astype(F32)[0:1]
    return whole * (jnp.exp(level * OCTAVE) * (1.0 / LEVELS))


def factor_tile(a):
    groups = TILE // SUB
    rows = lax.broadcasted_iota(jnp.int32, (SUB, TILE), 0)
    lanes = lax.broadcasted_iota(jnp.int32, (SUB, TILE), 1)
    left = [a[g * SUB : (g + 1) * SUB, :] for g in range(groups)]
    right = [jnp.where(lanes == rows + g * SUB, 1.0, 0.0).astype(F32) for g in range(groups)]
    spread = lambda x, j: jnp.broadcast_to(x[:, j : j + 1], (SUB, TILE))
    flat = lambda x, i: jnp.broadcast_to(x[i : i + 1, :], (SUB, TILE))
    column = [spread(x, 0) for x in left]
    pivots = [jnp.ones((SUB, TILE), F32) for _ in range(groups)]
    for j in range(TILE):
        g0, i0 = divmod(j, SUB)
        pivot = flat(column[g0], i0)
        pivots[g0] = jnp.where(rows == i0, pivot, pivots[g0])
        if j == TILE - 1:
            break
        inverse = 1.0 / pivot
        g1, i1 = divmod(j + 1, SUB)
        ahead = [spread(left[g], j + 1) if g >= g1 else None for g in range(groups)]
        corner = flat(column[g1], i1)
        left_row = flat(left[g0], i0)
        right_row = flat(right[g0], i0)
        following = [None] * groups
        for g in range(g0, groups):
            ratio = column[g] * inverse
            if g == g0:
                ratio = jnp.where(rows > i0, ratio, 0.0)
            if g >= g1:
                following[g] = ahead[g] - ratio * corner
            left[g] = left[g] - ratio * left_row
            right[g] = right[g] - ratio * right_row
        column = following
    return jnp.concatenate([r * lax.rsqrt(p) for r, p in zip(right, pivots)], axis=0)


def inverse_kernel(place_ref, *refs):
    *half_refs, x_ref, work, square = refs
    size = x_ref.shape[0]
    tiles = size // TILE
    owners = len(half_refs)
    width = size // owners
    core = place_ref[2]
    for s, half_ref in enumerate(half_refs):
        where = lax.rem(core + s, owners) * width
        square[:, pl.ds(pl.multiple_of(where, TILE), width)] = half_ref[...]
    rows = lax.broadcasted_iota(jnp.int32, (size, size), 0)
    columns = lax.broadcasted_iota(jnp.int32, (size, size), 1)
    value = square[...]
    work[...] = (value + value.T) * 0.5
    x_ref[...] = jnp.where(rows == columns, 1.0, 0.0).astype(F32)

    def step(p, carry):
        here = pl.ds(pl.multiple_of(p * TILE, TILE), TILE)
        tile = factor_tile(work[here, here])
        upper = jnp.dot(tile, work[here, :], precision=HI, preferred_element_type=F32)
        solved = jnp.dot(tile, x_ref[here, :], precision=HI, preferred_element_type=F32)
        x_ref[here, :] = solved
        for q in range(1, tiles):

            @pl.when(q > p)
            def _():
                below = slice(q * TILE, (q + 1) * TILE)
                part = upper[:, below]
                work[below, :] -= lax.dot_general(
                    part, upper, COLS_T, precision=HI, preferred_element_type=F32
                )
                x_ref[below, :] -= lax.dot_general(
                    part, solved, COLS_T, precision=HI, preferred_element_type=F32
                )

        return carry

    lax.fori_loop(0, tiles, step, 0)


def inverse_factor(place, halves):
    size = halves[0].shape[0]
    return pl.pallas_call(
        inverse_kernel,
        out_shape=shaped(size, size, F32),
        in_specs=[in_smem()] + in_vmem(len(halves)),
        out_specs=pl.BlockSpec(memory_space=pltpu.VMEM),
        scratch_shapes=[pltpu.VMEM((size, size), F32)] * 2,
        name="inverse_factor",
    )(place, *halves)


def weigh(rows_ref, primal_ref, dual_ref):
    rows = rows_ref[...]
    by_primal = jnp.dot(rows, primal_ref[...], preferred_element_type=F32).astype(BF16)
    by_dual = jnp.dot(rows, dual_ref[...], preferred_element_type=F32).astype(BF16)
    return by_primal, by_dual


def hadamard(by_primal, by_dual, columns):
    return lax.dot_general(
        by_primal, columns, ROWS_T, preferred_element_type=F32
    ) * lax.dot_general(by_dual, columns, ROWS_T, preferred_element_type=F32)


def pivot_kernel(place_ref, rows_ref, primal_ref, dual_ref, own_ref, code_ref, p_ref, d_ref):
    by_primal, by_dual = weigh(rows_ref, primal_ref, dual_ref)
    p_ref[...] = by_primal
    d_ref[...] = by_dual
    width = own_ref.shape[1]
    mine = pl.ds(pl.multiple_of(place_ref[2] * width, width), width)
    value = hadamard(by_primal, by_dual, rows_ref[mine, :])
    own_ref[...] = value
    for g in range(value.shape[0] // TILE):
        encode(value[g * TILE : (g + 1) * TILE], code_ref, g * (TILE + SUB))


def scatter_terms(value_ref, place_ref, own_ref, code_refs):
    share = own_ref.shape[0]
    cone = place_ref[0]
    own_ref[...] = value_ref[pl.ds(pl.multiple_of(cone * share, share), share), :]
    for u, code_ref in enumerate(code_refs, 1):
        other = jnp.bitwise_xor(cone, u) * share
        encode(value_ref[pl.ds(pl.multiple_of(other, share), share), :], code_ref, 0)


def panel_terms_kernel(place_ref, p_ref, d_ref, columns_ref, own_ref, *rest):
    *code_refs, value_ref = rest
    flag = place_ref[3].astype(F32)
    value_ref[...] = hadamard(p_ref[...], d_ref[...], columns_ref[...]) * flag
    scatter_terms(value_ref, place_ref, own_ref, code_refs)


def terms_kernel(place_ref, rows_ref, primal_ref, dual_ref, columns_ref, own_ref, *rest):
    *code_refs, value_ref = rest
    flag = place_ref[3].astype(F32)
    by_primal, by_dual = weigh(rows_ref, primal_ref, dual_ref)
    value_ref[...] = hadamard(by_primal, by_dual, columns_ref[...]) * flag
    scatter_terms(value_ref, place_ref, own_ref, code_refs)


def sum_half_kernel(own_ref, *refs):
    *code_refs, out_ref = refs
    for g in range(own_ref.shape[0] // TILE):
        rows = slice(g * TILE, (g + 1) * TILE)
        total = own_ref[rows, :]
        for code_ref in code_refs:
            total = total + decode(code_ref, g * (TILE + SUB), TILE)
        out_ref[rows, :] = total


def sum_panel_kernel(own_ref, *refs):
    *code_refs, sum_ref, out_ref = refs
    total = own_ref[...]
    for code_ref in code_refs:
        total = total + decode(code_ref, 0, total.shape[0])
    sum_ref[...] = total
    encode(total, out_ref, 0)


def sum_rest_kernel(cones, place_ref, *refs):
    blocks = cones - 1
    cone = place_ref[0]
    inputs = refs[: blocks * cones]
    own_ref, *code_refs = refs[blocks * cones : blocks * cones + cones]
    sums = refs[-1]
    for b in range(blocks):
        first, *codes = inputs[b * cones : (b + 1) * cones]
        total = first[...]
        for code in codes:
            total = total + decode(code, 0, total.shape[0])
        sums[b + 1] = total
    sums[0] = jnp.zeros_like(sums[0])
    own_ref[...] = sums[cone]
    for u, code_ref in enumerate(code_refs, 1):
        encode(sums[jnp.bitwise_xor(cone, u)], code_ref, 0)


def gather_panel_kernel(place_ref, own_ref, *refs):
    *code_refs, panel_ref, lead_ref = refs
    share = own_ref.shape[0]
    cone = place_ref[0]
    panel_ref[pl.ds(pl.multiple_of(cone * share, share), share), :] = own_ref[...]
    for u, code_ref in enumerate(code_refs, 1):
        other = jnp.bitwise_xor(cone, u) * share
        panel_ref[pl.ds(pl.multiple_of(other, share), share), :] = decode(code_ref, 0, share)
    width = lead_ref.shape[1]
    for g in range(panel_ref.shape[0] // TILE):
        encode(panel_ref[g * TILE : (g + 1) * TILE, :width], lead_ref, g * (TILE + SUB))


def rows_kernel(place_ref, inverse_ref, panel_ref, *refs):
    *lead_refs, factor_ref, row_ref, lead = refs
    owners = len(lead_refs)
    width = lead_refs[0].shape[1]
    core = place_ref[2]
    for s, lead_ref in enumerate(lead_refs):
        where = pl.ds(pl.multiple_of(lax.rem(core + s, owners) * width, width), width)
        for g in range(panel_ref.shape[0] // TILE):
            lead[g * TILE : (g + 1) * TILE, where] = decode(lead_ref, g * (TILE + SUB), TILE)
    inverse = inverse_ref[...]
    factor_ref[...] = jnp.dot(inverse, panel_ref[...], precision=HI, preferred_element_type=F32)
    row_ref[...] = jnp.dot(inverse, lead[...], precision=HI, preferred_element_type=F32)


def update_kernel(place_ref, factor_ref, row_ref, own_ref, *refs):
    *code_refs, out_ref = refs
    share = own_ref.shape[0]
    cone = place_ref[0]

    @pl.when(cone == 0)
    def _():
        out_ref[...] = factor_ref[...]

    @pl.when(cone != 0)
    def _():
        out_ref[pl.ds(pl.multiple_of(cone * share, share), share), :] = own_ref[...]
        for u, code_ref in enumerate(code_refs, 1):
            other = jnp.bitwise_xor(cone, u) * share
            out_ref[pl.ds(pl.multiple_of(other, share), share), :] = decode(code_ref, 0, share)
        change = lax.dot_general(
            row_ref[...], factor_ref[...], COLS_T, precision=HI, preferred_element_type=F32
        )
        columns = lax.broadcasted_iota(jnp.int32, out_ref.shape, 1)
        dropped = (columns < place_ref[5]) & (place_ref[4] != 0)
        out_ref[...] = jnp.where(dropped, 0.0, out_ref[...] - change)


def call(kernel, out_shape, place, operands, scratch=(), name=None):
    specs = in_vmem(len(operands))
    if place is not None:
        specs = [in_smem()] + specs
        operands = (place, *operands)
    return pl.pallas_call(
        kernel,
        out_shape=out_shape,
        in_specs=specs,
        out_specs=jax.tree.map(lambda _: pl.BlockSpec(memory_space=pltpu.VMEM), out_shape),
        scratch_shapes=scratch,
        name=name,
    )(*operands)


def shards(vectors, primal, dual_inverse, touches):
    con_count = lax.axis_size("con")
    cones = lax.axis_size("cone")
    con_place = lax.axis_index("con")
    cone_place = lax.axis_index("cone")
    per_block = vectors.shape[1]
    row_dev = PANEL * cones // con_count
    owners = con_count // cones
    share = PANEL // cones
    chip, core = con_place // owners, con_place % owners
    flag = lax.dynamic_index_in_dim(touches[0], con_place, 0, keepdims=False)
    place = jnp.stack(
        [
            cone_place,
            con_place,
            core,
            flag,
            (con_place < owners).astype(jnp.int32),
            jnp.int32(row_dev),
        ]
    ).astype(jnp.int32)
    columns, primal_block, dual_block = vectors[0], primal[0], dual_inverse[0]

    def across(value, u):
        return lax.ppermute(value, "cone", [(i, i ^ u) for i in range(cones)])

    def beside(value, s):
        pairs = [
            (g * owners + i, g * owners + (i - s) % owners)
            for g in range(cones)
            for i in range(owners)
        ]
        return lax.ppermute(value, "con", pairs)

    def exchange(codes):
        return [across(code, u) for u, code in enumerate(codes, 1)]

    own_rows = columns[:row_dev] * flag.astype(BF16)
    gathered = lax.all_gather(own_rows, "con", axis=0, tiled=True)
    blocks = [gathered[b * PANEL : (b + 1) * PANEL] for b in range(cones)]

    coded_square = (PANEL // TILE) * (TILE + SUB)
    half_own, half_code, by_primal, by_dual = call(
        pivot_kernel,
        (
            shaped(PANEL, row_dev, F32),
            shaped(coded_square, row_dev, I16),
            shaped(*blocks[0].shape, BF16),
            shaped(*blocks[0].shape, BF16),
        ),
        place,
        (blocks[0], primal_block, dual_block),
        name="pivot",
    )
    half_codes = [across(half_code, u) for u in range(1, cones)]

    terms_shape = (shaped(share, per_block, F32),) + (shaped(share + SUB, per_block, I16),) * (
        cones - 1
    )
    scratch = [pltpu.VMEM((PANEL, per_block), F32)]
    first, *codes = call(
        panel_terms_kernel, terms_shape, place, (by_primal, by_dual, columns), scratch, "panel_terms"
    )
    panel_parts = [first] + exchange(codes)
    rest_parts = []
    for b in range(1, cones):
        first, *codes = call(
            terms_kernel,
            terms_shape,
            place,
            (blocks[b], primal_block, dual_block, columns),
            scratch,
            f"terms_{b}",
        )
        rest_parts += [first] + exchange(codes)

    half = call(
        sum_half_kernel, shaped(PANEL, row_dev, F32), None, (half_own, *half_codes), name="sum_half"
    )
    halves = [half] + [beside(half, s) for s in range(1, owners)]
    inverse = inverse_factor(place, halves)

    panel_own, panel_code = call(
        sum_panel_kernel,
        (shaped(share, per_block, F32), shaped(share + SUB, per_block, I16)),
        None,
        panel_parts,
        name="sum_panel",
    )
    panel_codes = [across(panel_code, u) for u in range(1, cones)]
    panel, lead = call(
        gather_panel_kernel,
        (shaped(PANEL, per_block, F32), shaped(coded_square, row_dev, I16)),
        place,
        (panel_own, *panel_codes),
        name="gather_panel",
    )
    mine = jnp.where(chip == cone_place, lead, jnp.zeros_like(lead))
    for d in range(1, cones):
        pairs = [
            (c * con_count + c * owners + i, c * con_count + (c ^ d) * owners + i)
            for c in range(1, cones)
            for i in range(owners)
        ]
        mine = mine + lax.ppermute(lead, ("cone", "con"), pairs)
    leads = [mine] + [beside(mine, s) for s in range(1, owners)]


    rest_own, *rest_codes = call(
        functools.partial(sum_rest_kernel, cones),
        terms_shape,
        place,
        rest_parts,
        [pltpu.VMEM((cones, share, per_block), F32)],
        "sum_rest",
    )
    rest_codes = [
        lax.ppermute(code, "cone", [(i, i ^ u) for i in range(cones) if i ^ u])
        for u, code in enumerate(rest_codes, 1)
    ]
    factor_rows, row_factor = call(
        rows_kernel,
        (shaped(PANEL, per_block, F32), shaped(PANEL, PANEL, F32)),
        place,
        (inverse, panel, *leads),
        [pltpu.VMEM((PANEL, PANEL), F32)],
        "rows",
    )
    return call(
        update_kernel,
        shaped(PANEL, per_block, F32),
        place,
        (factor_rows, row_factor, rest_own, *rest_codes),
        name="update",
    )


def solution(mesh):
    in_specs = (
        P("cone", "con", None),
        P("cone", None, None),
        P("cone", None, None),
        P("cone", None),
    )
    out_specs = P("cone", "con")
    return jax.shard_map(shards, mesh=mesh, in_specs=in_specs, out_specs=out_specs, check_vma=False)
```

```python
import functools
import math

import jax
import jax.numpy as jnp
from jax import lax
from jax.experimental import pallas as pl
from jax.experimental.pallas import tpu as pltpu
from jax.sharding import PartitionSpec as P


PANEL = 512
TILE = 128
SUB = 8
STEPS = 128
LEVELS = 32767.0
OCTAVE = math.log(2.0) / STEPS
HI = lax.Precision.HIGHEST
ROWS_T = (((1,), (1,)), ((), ()))
COLS_T = (((0,), (0,)), ((), ()))
PLAIN = (((1,), (0,)), ((), ()))
F32 = jnp.float32
BF16 = jnp.bfloat16
I16 = jnp.int16


def in_vmem(count):
    return [pl.BlockSpec(memory_space=pltpu.VMEM)] * count


def in_smem():
    return pl.BlockSpec(memory_space=pltpu.SMEM)


def shaped(rows, columns, dtype):
    return jax.ShapeDtypeStruct((rows, columns), dtype)


def encode(value, out_ref, start):
    rows = value.shape[0]
    top = jnp.max(jnp.abs(value), axis=0, keepdims=True)
    level = jnp.ceil(jnp.log(jnp.maximum(top, 1e-37)) * (1.0 / OCTAVE))
    scaled = value * jnp.exp(level * -OCTAVE) * LEVELS
    whole = jnp.round(jnp.clip(scaled, -LEVELS, LEVELS)).astype(jnp.int32)
    out_ref[start : start + rows, :] = whole.astype(I16)
    levels = jnp.broadcast_to(level, (SUB, value.shape[1])).astype(jnp.int32)
    out_ref[start + rows : start + rows + SUB, :] = levels.astype(I16)


def decode(ref, start, rows):
    whole = ref[start : start + rows, :].astype(jnp.int32).astype(F32)
    level = ref[start + rows : start + rows + SUB, :].astype(jnp.int32).astype(F32)[0:1]
    return whole * (jnp.exp(level * OCTAVE) * (1.0 / LEVELS))


def factor_tile(a):
    groups = TILE // SUB
    rows = lax.broadcasted_iota(jnp.int32, (SUB, TILE), 0)
    lanes = lax.broadcasted_iota(jnp.int32, (SUB, TILE), 1)
    left = [a[g * SUB : (g + 1) * SUB, :] for g in range(groups)]
    right = [jnp.where(lanes == rows + g * SUB, 1.0, 0.0).astype(F32) for g in range(groups)]
    spread = lambda x, j: jnp.broadcast_to(x[:, j : j + 1], (SUB, TILE))
    flat = lambda x, i: jnp.broadcast_to(x[i : i + 1, :], (SUB, TILE))
    column = [spread(x, 0) for x in left]
    pivots = [jnp.ones((SUB, TILE), F32) for _ in range(groups)]
    for j in range(TILE):
        g0, i0 = divmod(j, SUB)
        pivot = flat(column[g0], i0)
        pivots[g0] = jnp.where(rows == i0, pivot, pivots[g0])
        if j == TILE - 1:
            break
        inverse = 1.0 / pivot
        g1, i1 = divmod(j + 1, SUB)
        ahead = [spread(left[g], j + 1) if g >= g1 else None for g in range(groups)]
        corner = flat(column[g1], i1)
        left_row = flat(left[g0], i0)
        right_row = flat(right[g0], i0)
        following = [None] * groups
        for g in range(g0, groups):
            ratio = column[g] * inverse
            if g == g0:
                ratio = jnp.where(rows > i0, ratio, 0.0)
            if g >= g1:
                following[g] = ahead[g] - ratio * corner
            left[g] = left[g] - ratio * left_row
            right[g] = right[g] - ratio * right_row
        column = following
    return jnp.concatenate([r * lax.rsqrt(p) for r, p in zip(right, pivots)], axis=0)


def eliminate_kernel(first, last, work_in, x_in, work, x_ref):
    del work_in, x_in
    tiles = work.shape[0] // TILE

    def step(p, carry):
        here = pl.ds(pl.multiple_of(p * TILE, TILE), TILE)
        tile = factor_tile(work[here, here])
        upper = jnp.dot(tile, work[here, :], precision=HI, preferred_element_type=F32)
        solved = jnp.dot(tile, x_ref[here, :], precision=HI, preferred_element_type=F32)
        x_ref[here, :] = solved
        for q in range(first + 1, tiles):

            @pl.when(q > p)
            def _():
                below = slice(q * TILE, (q + 1) * TILE)
                part = upper[:, below]
                work[below, :] -= lax.dot_general(
                    part, upper, COLS_T, precision=HI, preferred_element_type=F32
                )
                x_ref[below, :] -= lax.dot_general(
                    part, solved, COLS_T, precision=HI, preferred_element_type=F32
                )

        return carry

    lax.fori_loop(first, last, step, 0)


def eliminate(work, x, first, last):
    size = work.shape[0]
    return pl.pallas_call(
        functools.partial(eliminate_kernel, first, last),
        out_shape=(shaped(size, size, F32),) * 2,
        in_specs=in_vmem(2),
        out_specs=tuple(in_vmem(2)),
        input_output_aliases={0: 0, 1: 1},
        compiler_params=pltpu.CompilerParams(vmem_limit_bytes=6 << 20),
    )(work, x)


def square_kernel(*refs):
    *half_refs, work, x_ref, square = refs
    size = x_ref.shape[0]
    owners = len(half_refs)
    width = size // owners
    core = lax.rem(lax.axis_index("con"), owners)
    for s, half_ref in enumerate(half_refs):
        where = lax.rem(core + s, owners) * width
        square[:, pl.ds(pl.multiple_of(where, TILE), width)] = half_ref[...]
    rows = lax.broadcasted_iota(jnp.int32, (size, size), 0)
    columns = lax.broadcasted_iota(jnp.int32, (size, size), 1)
    value = square[...]
    work[...] = (value + value.T) * 0.5
    x_ref[...] = jnp.where(rows == columns, 1.0, 0.0).astype(F32)


def hadamard(rows, primal_ref, dual_ref, columns):
    by_primal = jnp.dot(rows, primal_ref[...], preferred_element_type=F32).astype(BF16)
    by_dual = jnp.dot(rows, dual_ref[...], preferred_element_type=F32).astype(BF16)
    return lax.dot_general(
        by_primal, columns, ROWS_T, preferred_element_type=F32
    ) * lax.dot_general(by_dual, columns, ROWS_T, preferred_element_type=F32)


def split(value):
    high = value.astype(BF16)
    return high, (value - high.astype(F32)).astype(BF16)


def product(left, right, contract):
    dot = functools.partial(
        lax.dot_general, dimension_numbers=contract, preferred_element_type=F32
    )
    left_high, left_low = left
    right_high, right_low = right
    return dot(left_high, right_high) + (dot(left_high, right_low) + dot(left_low, right_high))


def mask_kernel(touches_ref, rows_ref, out_ref):
    flag = touches_ref[0, lax.axis_index("con")]
    out_ref[...] = rows_ref[...] * flag.astype(BF16)


def pick_kernel(owners, chips, *refs):
    *in_refs, out_ref = refs
    chip = lax.div(lax.axis_index("con"), owners)
    for in_ref, members in zip(in_refs, chips):
        for member in members:

            @pl.when(chip == member)
            def _():
                out_ref[...] = in_ref[...]


def assemble(part_refs, rows):
    owners = len(part_refs)
    count = part_refs[0].shape[0]
    core = lax.rem(lax.axis_index("con"), owners)
    for s, part_ref in enumerate(part_refs):
        where = pl.multiple_of(lax.rem(core + s, owners) * count, count)
        rows[pl.ds(where, count), :] = part_ref[...]


def panel_step(chip):
    return jnp.minimum(chip, 2)


def pivot_kernel(owners, steps, *refs):
    groups = [refs[s * owners : (s + 1) * owners] for s in range(steps)]
    primal_ref, dual_ref, own_ref, code_ref, rows, columns = refs[steps * owners :]
    step = panel_step(lax.div(lax.axis_index("con"), owners))
    for s, part_refs in enumerate(groups):

        @pl.when(step == s)
        def _():
            assemble(part_refs, rows)
            columns[...] = part_refs[0][...]

    value = hadamard(rows[...], primal_ref, dual_ref, columns[...])
    own_ref[...] = value
    for g in range(value.shape[0] // TILE):
        encode(value[g * TILE : (g + 1) * TILE], code_ref, g * (TILE + SUB))


def terms_kernel(owners, touches_ref, *refs):
    part_refs = refs[:owners]
    primal_ref, dual_ref, columns_ref, own_ref, *code_refs, rows, value_ref = refs[owners:]
    assemble(part_refs, rows)
    flag = touches_ref[0, lax.axis_index("con")].astype(F32)
    value_ref[...] = hadamard(rows[...], primal_ref, dual_ref, columns_ref[...]) * flag
    share = own_ref.shape[0]
    cone = lax.axis_index("cone")
    own_ref[...] = value_ref[pl.ds(pl.multiple_of(cone * share, share), share), :]
    for u, code_ref in enumerate(code_refs, 1):
        other = jnp.bitwise_xor(cone, u) * share
        encode(value_ref[pl.ds(pl.multiple_of(other, share), share), :], code_ref, 0)


def sum_half_kernel(own_ref, *refs):
    *code_refs, out_ref = refs
    for g in range(own_ref.shape[0] // TILE):
        rows = slice(g * TILE, (g + 1) * TILE)
        total = own_ref[rows, :]
        for code_ref in code_refs:
            total = total + decode(code_ref, g * (TILE + SUB), TILE)
        out_ref[rows, :] = total


def total_of(own_ref, code_refs):
    total = own_ref[...]
    for code_ref in code_refs:
        total = total + decode(code_ref, 0, total.shape[0])
    return total


def sum_panel_kernel(owners, cones, steps, *refs):
    sum_ref, out_ref = refs[-2:]
    step = panel_step(lax.div(lax.axis_index("con"), owners))
    for s in range(steps):

        @pl.when(step == s)
        def _():
            total = total_of(refs[s * cones], refs[s * cones + 1 : (s + 1) * cones])
            sum_ref[...] = total
            encode(total, out_ref, 0)


def sum_rest_kernel(owners, cones, order_ref, *refs):
    cone = lax.axis_index("cone")
    chip = lax.div(lax.axis_index("con"), owners)
    inputs = refs[: cones * cones]
    own_ref, *code_refs = refs[cones * cones : cones * cones + cones]
    sums = refs[-1]
    for s in range(cones):
        block = order_ref[chip, s]

        @pl.when(block != 0)
        def _():
            sums[block] = total_of(inputs[s * cones], inputs[s * cones + 1 : (s + 1) * cones])

    @pl.when(cone != 0)
    def _():
        own_ref[...] = sums[cone]

    for u, code_ref in enumerate(code_refs, 1):
        other = jnp.bitwise_xor(cone, u)

        @pl.when(other != 0)
        def _():
            encode(sums[other], code_ref, 0)


def gather_panel_kernel(own_ref, *refs):
    *code_refs, panel_ref, lead_ref = refs
    share = own_ref.shape[0]
    cone = lax.axis_index("cone")
    panel_ref[pl.ds(pl.multiple_of(cone * share, share), share), :] = own_ref[...]
    for u, code_ref in enumerate(code_refs, 1):
        other = jnp.bitwise_xor(cone, u) * share
        panel_ref[pl.ds(pl.multiple_of(other, share), share), :] = decode(code_ref, 0, share)
    width = lead_ref.shape[1]
    for g in range(panel_ref.shape[0] // TILE):
        encode(panel_ref[g * TILE : (g + 1) * TILE, :width], lead_ref, g * (TILE + SUB))


def pick_lead_kernel(owners, *refs):
    *in_refs, out_ref = refs
    chip = lax.div(lax.axis_index("con"), owners)
    step = jnp.bitwise_xor(chip, lax.axis_index("cone"))
    for d, in_ref in enumerate(in_refs):

        @pl.when(step == d)
        def _():
            out_ref[...] = in_ref[...]


def rows_kernel(inverse_ref, panel_ref, *refs):
    *lead_refs, factor_ref, row_ref, lead = refs
    owners = len(lead_refs)
    width = lead_refs[0].shape[1]
    core = lax.rem(lax.axis_index("con"), owners)
    for s, lead_ref in enumerate(lead_refs):
        where = pl.ds(pl.multiple_of(lax.rem(core + s, owners) * width, width), width)
        for g in range(panel_ref.shape[0] // TILE):
            lead[g * TILE : (g + 1) * TILE, where] = decode(lead_ref, g * (TILE + SUB), TILE)
    inverse = split(inverse_ref[...])
    factor_ref[...] = product(inverse, split(panel_ref[...]), PLAIN)
    row_ref[...] = product(inverse, split(lead[...]), PLAIN)


def update_kernel(owners, width, factor_ref, row_ref, own_ref, *refs):
    *code_refs, out_ref = refs
    share = own_ref.shape[0]
    cone = lax.axis_index("cone")
    pivots = lax.axis_index("con") < owners

    @pl.when(cone == 0)
    def _():
        out_ref[...] = factor_ref[...]

    @pl.when(cone != 0)
    def _():
        out_ref[pl.ds(pl.multiple_of(cone * share, share), share), :] = own_ref[...]
        for u, code_ref in enumerate(code_refs, 1):
            other = jnp.bitwise_xor(cone, u) * share
            out_ref[pl.ds(pl.multiple_of(other, share), share), :] = decode(code_ref, 0, share)
        change = product(split(row_ref[...]), split(factor_ref[...]), COLS_T)
        columns = lax.broadcasted_iota(jnp.int32, out_ref.shape, 1)
        out_ref[...] = jnp.where((columns < width) & pivots, 0.0, out_ref[...] - change)


def call(kernel, out_shape, operands, scratch=(), limit=16, scalars=0):
    return pl.pallas_call(
        kernel,
        out_shape=out_shape,
        in_specs=[in_smem()] * scalars + in_vmem(len(operands) - scalars),
        out_specs=jax.tree.map(lambda _: pl.BlockSpec(memory_space=pltpu.VMEM), out_shape),
        scratch_shapes=scratch,
        compiler_params=pltpu.CompilerParams(vmem_limit_bytes=limit << 20),
    )(*operands)


def arrival(chip, block, chips):
    d = chip ^ block
    return (-1, 1) if d == 1 else (min(block, chips - 1 - block), d)


def block_order(chip, chips):
    rest = [b for b in range(chips) if b not in (chip, chip ^ 1)]
    key = lambda b: (arrival(chip, b, chips)[0], b != 0, -arrival(chip, b, chips)[1])
    return [chip, chip ^ 1] + sorted(rest, key=key)


def gather_keys(chips):
    phases = range(chips // 2)
    return [(-1, 1)] + [(p, d) for p in phases for d in reversed(range(2, chips))]


def shards(vectors, primal, dual_inverse, touches):
    con_count = lax.axis_size("con")
    cones = lax.axis_size("cone")
    per_block, order_n = vectors.shape[1:]
    row_dev = PANEL * cones // con_count
    owners = con_count // cones
    share = PANEL // cones
    steps = min(cones, 3)
    columns, primal_block, dual_block = vectors[0], primal[0], dual_inverse[0]
    order = [block_order(z, cones) for z in range(cones)]

    def exchange(codes, pairs=lambda u: [(i, i ^ u) for i in range(cones)]):
        return [lax.ppermute(code, "cone", pairs(u)) for u, code in enumerate(codes, 1)]

    def along(value, moves):
        pairs = [(a * owners + i, b * owners + i) for a, b in moves for i in range(owners)]
        return lax.ppermute(value, "con", pairs)

    def beside(value):
        swaps = [value]
        for s in range(1, owners):
            pairs = [
                (g * owners + i, g * owners + (i - s) % owners)
                for g in range(cones)
                for i in range(owners)
            ]
            swaps.append(lax.ppermute(value, "con", pairs))
        return swaps

    own_rows = pl.pallas_call(
        mask_kernel,
        grid=(1,),
        out_shape=shaped(row_dev, order_n, BF16),
        in_specs=[in_smem(), pl.BlockSpec((row_dev, order_n), lambda i: (0, 0))],
        out_specs=pl.BlockSpec((row_dev, order_n), lambda i: (0, 0)),
        compiler_params=pltpu.CompilerParams(vmem_limit_bytes=4 << 20),
        name="mask_rows",
    )(touches, columns)
    parts = [beside(own_rows)]
    arrived = {}
    for phase, d in gather_keys(cones):
        sources = range(cones) if phase < 0 else sorted({phase, cones - 1 - phase})
        moves = [(b, b ^ d) for b in sources]
        arrived[phase, d] = along(own_rows, moves)

    for step in range(1, cones):
        wanted = {}
        for z in range(cones):
            wanted.setdefault(arrival(z, order[z][step], cones), []).append(z)
        keys = sorted(wanted)
        mine = call(
            functools.partial(pick_kernel, owners, [wanted[key] for key in keys]),
            shaped(row_dev, order_n, BF16),
            tuple(arrived[key] for key in keys),
            limit=4,
        )
        parts.append(beside(mine))

    terms_shape = (shaped(share, per_block, F32),) + (shaped(share + SUB, per_block, I16),) * (
        cones - 1
    )
    summed = []
    for step in range(cones):
        first, *codes = call(
            functools.partial(terms_kernel, owners),
            terms_shape,
            (touches, *parts[step], primal_block, dual_block, columns),
            [pltpu.VMEM((PANEL, order_n), BF16), pltpu.VMEM((PANEL, per_block), F32)],
            16,
            1,
        )
        summed.append([first] + exchange(codes))

    coded_square = (PANEL // TILE) * (TILE + SUB)
    half_own, half_code = call(
        functools.partial(pivot_kernel, owners, steps),
        (shaped(PANEL, row_dev, F32), shaped(coded_square, row_dev, I16)),
        (*[part for group in parts[:steps] for part in group], primal_block, dual_block),
        [pltpu.VMEM((PANEL, order_n), BF16), pltpu.VMEM((row_dev, order_n), BF16)],
        16,
    )
    half_codes = exchange([half_code] * (cones - 1))
    half = call(sum_half_kernel, shaped(PANEL, row_dev, F32), (half_own, *half_codes), limit=4)
    work, inverse = call(
        square_kernel,
        (shaped(PANEL, PANEL, F32),) * 2,
        tuple(beside(half)),
        [pltpu.VMEM((PANEL, PANEL), F32)],
        6,
    )
    tiles = PANEL // TILE
    work, inverse = eliminate(work, inverse, 0, tiles // 2)
    work, inverse = eliminate(work, inverse, tiles // 2, tiles)

    panel_own, panel_code = call(
        functools.partial(sum_panel_kernel, owners, cones, steps),
        (shaped(share, per_block, F32), shaped(share + SUB, per_block, I16)),
        tuple(part for group in summed[:steps] for part in group),
        limit=8,
    )
    panel, lead = call(
        gather_panel_kernel,
        (shaped(PANEL, per_block, F32), shaped(coded_square, row_dev, I16)),
        (panel_own, *exchange([panel_code] * (cones - 1))),
        limit=6,
    )
    leads = [lead]
    for d in range(1, cones):
        pairs = [
            (c * con_count + c * owners + i, c * con_count + (c ^ d) * owners + i)
            for c in range(1, cones)
            for i in range(owners)
        ]
        leads.append(lax.ppermute(lead, ("cone", "con"), pairs))
    lead = call(
        functools.partial(pick_lead_kernel, owners),
        shaped(coded_square, row_dev, I16),
        tuple(leads),
        limit=4,
    )
    rest_own, *rest_codes = call(
        functools.partial(sum_rest_kernel, owners, cones),
        terms_shape,
        (jnp.array(order, jnp.int32), *[part for group in summed for part in group]),
        [pltpu.VMEM((cones, share, per_block), F32)],
        16,
        1,
    )
    rest_codes = exchange(rest_codes, lambda u: [(i, i ^ u) for i in range(cones) if i ^ u])
    factor_rows, row_factor = call(
        rows_kernel,
        (shaped(PANEL, per_block, F32), shaped(PANEL, PANEL, F32)),
        (inverse, panel, *beside(lead)),
        [pltpu.VMEM((PANEL, PANEL), F32)],
        14,
    )
    return call(
        functools.partial(update_kernel, owners, row_dev),
        shaped(PANEL, per_block, F32),
        (factor_rows, row_factor, rest_own, *rest_codes),
        limit=14,
    )


def solution(mesh):
    in_specs = (
        P("cone", "con", None),
        P("cone", None, None),
        P("cone", None, None),
        P("cone", None),
    )
    out_specs = P("cone", "con")

    return jax.shard_map(shards, mesh=mesh, in_specs=in_specs, out_specs=out_specs, check_vma=False)
```

```python
import functools
import math

import jax
import jax.numpy as jnp
from jax import lax
from jax.experimental import pallas as pl
from jax.experimental.pallas import tpu as pltpu
from jax.sharding import PartitionSpec as P


PANEL = 512
TILE = 128
SUB = 8
STEPS = 128
LEVELS = 32767.0
OCTAVE = math.log(2.0) / STEPS
HI = lax.Precision.HIGHEST
ROWS_T = (((1,), (1,)), ((), ()))
COLS_T = (((0,), (0,)), ((), ()))
PLAIN = (((1,), (0,)), ((), ()))
F32 = jnp.float32
BF16 = jnp.bfloat16
I16 = jnp.int16


def in_vmem(count):
    return [pl.BlockSpec(memory_space=pltpu.VMEM)] * count


def in_smem():
    return pl.BlockSpec(memory_space=pltpu.SMEM)


def shaped(rows, columns, dtype):
    return jax.ShapeDtypeStruct((rows, columns), dtype)


def encode(value, out_ref, start):
    rows = value.shape[0]
    top = jnp.max(jnp.abs(value), axis=0, keepdims=True)
    level = jnp.ceil(jnp.log(jnp.maximum(top, 1e-37)) * (1.0 / OCTAVE))
    scaled = value * jnp.exp(level * -OCTAVE) * LEVELS
    whole = jnp.round(jnp.clip(scaled, -LEVELS, LEVELS)).astype(jnp.int32)
    out_ref[start : start + rows, :] = whole.astype(I16)
    levels = jnp.broadcast_to(level, (SUB, value.shape[1])).astype(jnp.int32)
    out_ref[start + rows : start + rows + SUB, :] = levels.astype(I16)


def decode(ref, start, rows):
    whole = ref[start : start + rows, :].astype(jnp.int32).astype(F32)
    level = ref[start + rows : start + rows + SUB, :].astype(jnp.int32).astype(F32)[0:1]
    return whole * (jnp.exp(level * OCTAVE) * (1.0 / LEVELS))


def factor_tile(a):
    groups = TILE // SUB
    rows = lax.broadcasted_iota(jnp.int32, (SUB, TILE), 0)
    lanes = lax.broadcasted_iota(jnp.int32, (SUB, TILE), 1)
    left = [a[g * SUB : (g + 1) * SUB, :] for g in range(groups)]
    right = [jnp.where(lanes == rows + g * SUB, 1.0, 0.0).astype(F32) for g in range(groups)]
    spread = lambda x, j: jnp.broadcast_to(x[:, j : j + 1], (SUB, TILE))
    flat = lambda x, i: jnp.broadcast_to(x[i : i + 1, :], (SUB, TILE))
    first = [spread(x, 0) for x in left]
    second = [spread(x, 1) for x in left]
    scales = [None] * groups
    for j in range(0, TILE, 2):
        g0, i0 = divmod(j, SUB)
        corner, side, end = flat(first[g0], i0), flat(first[g0], i0 + 1), flat(second[g0], i0 + 1)
        by_first = 1.0 / corner
        by_second = corner * (1.0 / (corner * end - side * side))
        slope = side * by_first
        scale = jnp.where(rows == i0, by_first, by_second)
        scales[g0] = scale if i0 == 0 else jnp.where(rows >= i0, scale, scales[g0])
        left_0, right_0 = flat(left[g0], i0), flat(right[g0], i0)
        left_1 = flat(left[g0], i0 + 1) - slope * left_0
        right_1 = flat(right[g0], i0 + 1) - slope * right_0
        more = j + 2 < TILE
        if more:
            g1, i1 = divmod(j + 2, SUB)
            ahead_0 = [spread(left[g], j + 2) if g >= g1 else None for g in range(groups)]
            ahead_1 = [spread(left[g], j + 3) if g >= g1 else None for g in range(groups)]
            p0, q0 = flat(first[g1], i1), flat(first[g1], i1 + 1)
            p1 = flat(second[g1], i1) - slope * p0
            q1 = flat(second[g1], i1 + 1) - slope * q0
        following = [None] * groups, [None] * groups
        for g in range(g0, groups):
            ratio_0 = first[g] * by_first
            ratio_1 = (second[g] - first[g] * slope) * by_second
            if g == g0:
                ratio_0 = jnp.where(rows > i0, ratio_0, 0.0)
                ratio_1 = jnp.where(rows > i0 + 1, ratio_1, 0.0)
            if more and g >= g1:
                following[0][g] = (ahead_0[g] - ratio_0 * p0) - ratio_1 * p1
                following[1][g] = (ahead_1[g] - ratio_0 * q0) - ratio_1 * q1
            left[g] = (left[g] - ratio_0 * left_0) - ratio_1 * left_1
            right[g] = (right[g] - ratio_0 * right_0) - ratio_1 * right_1
        first, second = following
    return jnp.concatenate([r * jnp.sqrt(p) for r, p in zip(right, scales)], axis=0)


def eliminate_kernel(first, last, work_in, x_in, work, x_ref):
    del work_in, x_in
    tiles = work.shape[0] // TILE

    def step(p, carry):
        here = pl.ds(pl.multiple_of(p * TILE, TILE), TILE)
        tile = factor_tile(work[here, here])
        upper = jnp.dot(tile, work[here, :], precision=HI, preferred_element_type=F32)
        solved = jnp.dot(tile, x_ref[here, :], precision=HI, preferred_element_type=F32)
        x_ref[here, :] = solved
        for q in range(first + 1, tiles):

            @pl.when(q > p)
            def _():
                below = slice(q * TILE, (q + 1) * TILE)
                part = upper[:, below]
                work[below, :] -= lax.dot_general(
                    part, upper, COLS_T, precision=HI, preferred_element_type=F32
                )
                x_ref[below, :] -= lax.dot_general(
                    part, solved, COLS_T, precision=HI, preferred_element_type=F32
                )

        return carry

    lax.fori_loop(first, last, step, 0)


def eliminate(work, x, first, last):
    size = work.shape[0]
    return pl.pallas_call(
        functools.partial(eliminate_kernel, first, last),
        out_shape=(shaped(size, size, F32),) * 2,
        in_specs=in_vmem(2),
        out_specs=tuple(in_vmem(2)),
        input_output_aliases={0: 0, 1: 1},
        compiler_params=pltpu.CompilerParams(vmem_limit_bytes=6 << 20),
    )(work, x)


def square_kernel(*refs):
    *half_refs, work, x_ref, square = refs
    size = x_ref.shape[0]
    owners = len(half_refs)
    width = size // owners
    core = lax.rem(lax.axis_index("con"), owners)
    for s, half_ref in enumerate(half_refs):
        where = lax.rem(core + s, owners) * width
        at = pl.ds(pl.multiple_of(where, TILE), width)
        for g in range(size // TILE):
            square[g * TILE : (g + 1) * TILE, at] = decode(half_ref, g * (TILE + SUB), TILE)
    rows = lax.broadcasted_iota(jnp.int32, (size, size), 0)
    columns = lax.broadcasted_iota(jnp.int32, (size, size), 1)
    value = square[...]
    value = (value + value.T) * 0.5
    diagonal = jnp.where(rows == columns, value, 0.0)
    across = lax.rsqrt(jnp.sum(diagonal, axis=0, keepdims=True))
    down = lax.rsqrt(jnp.sum(diagonal, axis=1, keepdims=True))
    work[...] = value * across * down
    x_ref[...] = jnp.where(rows == columns, across, 0.0)


def weigh(rows_ref, primal_ref, dual_ref, by_primal, by_dual):
    def part(i, carry):
        half = primal_ref.shape[1] // 2
        at = pl.ds(pl.multiple_of(i * half, half), half)
        for source, target in ((primal_ref, by_primal), (dual_ref, by_dual)):
            value = jnp.dot(rows_ref[...], source[:, at], preferred_element_type=F32)
            target[:, at] = value.astype(BF16)
        return carry

    lax.fori_loop(0, 2, part, 0)


def hadamard(by_primal, by_dual, columns):
    return lax.dot_general(
        by_primal, columns, ROWS_T, preferred_element_type=F32
    ) * lax.dot_general(by_dual, columns, ROWS_T, preferred_element_type=F32)


def split(value):
    high = value.astype(BF16)
    return high, (value - high.astype(F32)).astype(BF16)


def product(left, right, contract):
    dot = functools.partial(
        lax.dot_general, dimension_numbers=contract, preferred_element_type=F32
    )
    left_high, left_low = left
    right_high, right_low = right
    return dot(left_high, right_high) + (dot(left_high, right_low) + dot(left_low, right_high))


def mask_kernel(touches_ref, rows_ref, out_ref, flags, arrived):
    count = out_ref.shape[0]
    copies = [
        pltpu.make_async_copy(touches_ref, flags, arrived.at[0]),
        pltpu.make_async_copy(rows_ref.at[pl.ds(0, count), :], out_ref, arrived.at[1]),
    ]
    for copy in copies:
        copy.start()
    for copy in copies:
        copy.wait()
    out_ref[...] = out_ref[...] * flags[0, lax.axis_index("con")].astype(BF16)


def pick_kernel(owners, chips, *refs):
    *in_refs, out_ref = refs
    chip = lax.div(lax.axis_index("con"), owners)
    for in_ref, members in zip(in_refs, chips):
        for member in members:

            @pl.when(chip == member)
            def _():
                out_ref[...] = in_ref[...]


def assemble(part_refs, rows):
    owners = len(part_refs)
    count = part_refs[0].shape[0]
    core = lax.rem(lax.axis_index("con"), owners)
    for s, part_ref in enumerate(part_refs):
        where = pl.multiple_of(lax.rem(core + s, owners) * count, count)
        rows[pl.ds(where, count), :] = part_ref[...]


def panel_step(chip):
    return jnp.minimum(chip, 2)


def terms_kernel(owners, cones, touches_ref, *refs):
    part_refs = refs[:owners]
    primal_ref, dual_ref, columns_ref, own_ref = refs[owners : owners + 4]
    code_refs = refs[owners + 4 : owners + 3 + cones]
    lead_refs = refs[owners + 3 + cones : -4]
    rows, value_ref, p_ref, d_ref = refs[-4:]
    assemble(part_refs, rows)
    weigh(rows, primal_ref, dual_ref, p_ref, d_ref)
    flag = touches_ref[0, lax.axis_index("con")].astype(F32)
    value_ref[...] = hadamard(p_ref[...], d_ref[...], columns_ref[...]) * flag
    share = own_ref.shape[0]
    cone = lax.axis_index("cone")
    own_ref[...] = value_ref[pl.ds(pl.multiple_of(cone * share, share), share), :]
    for u, code_ref in enumerate(code_refs, 1):
        other = jnp.bitwise_xor(cone, u) * share
        encode(value_ref[pl.ds(pl.multiple_of(other, share), share), :], code_ref, 0)
    if lead_refs:
        lead_ref, lead_code_ref = lead_refs
        value = value_ref[:, : lead_ref.shape[1]]
        lead_ref[...] = value
        encode_square(value, lead_code_ref)


def encode_square(value, code_ref):
    for g in range(value.shape[0] // TILE):
        encode(value[g * TILE : (g + 1) * TILE], code_ref, g * (TILE + SUB))


def sum_half_kernel(own_ref, *refs):
    *code_refs, out_ref = refs
    for g in range(own_ref.shape[0] // TILE):
        total = own_ref[g * TILE : (g + 1) * TILE, :]
        for code_ref in code_refs:
            total = total + decode(code_ref, g * (TILE + SUB), TILE)
        encode(total, out_ref, g * (TILE + SUB))


def total_of(parts):
    own_ref, *code_refs = parts
    total = own_ref[...]
    for code_ref in code_refs:
        total = total + decode(code_ref, 0, total.shape[0])
    return total


def sum_panel_kernel(owners, cones, steps, *refs):
    sum_ref, out_ref = refs[-2:]
    step = panel_step(lax.div(lax.axis_index("con"), owners))
    for s in range(steps):

        @pl.when(step == s)
        def _():
            total = total_of(refs[s * cones : (s + 1) * cones])
            sum_ref[...] = total
            encode(total, out_ref, 0)


def sum_rest_kernel(owners, cones, order_ref, *refs):
    cone = lax.axis_index("cone")
    chip = lax.div(lax.axis_index("con"), owners)
    inputs = refs[: cones * cones]
    own_ref, *code_refs = refs[cones * cones : cones * cones + cones]
    sums = refs[-1]
    for s in range(cones):
        block = order_ref[chip, s]

        @pl.when(block != 0)
        def _():
            sums[block] = total_of(inputs[s * cones : (s + 1) * cones])

    @pl.when(cone != 0)
    def _():
        own_ref[...] = sums[cone]

    for u, code_ref in enumerate(code_refs, 1):
        other = jnp.bitwise_xor(cone, u)

        @pl.when(other != 0)
        def _():
            encode(sums[other], code_ref, 0)


def gather_panel_kernel(own_ref, *refs):
    *code_refs, panel_ref, lead_ref = refs
    share = own_ref.shape[0]
    cone = lax.axis_index("cone")
    panel_ref[pl.ds(pl.multiple_of(cone * share, share), share), :] = own_ref[...]
    for u, code_ref in enumerate(code_refs, 1):
        other = jnp.bitwise_xor(cone, u) * share
        panel_ref[pl.ds(pl.multiple_of(other, share), share), :] = decode(code_ref, 0, share)
    width = lead_ref.shape[1]
    encode_square(panel_ref[:, :width], lead_ref)


def pick_lead_kernel(owners, *refs):
    *in_refs, out_ref = refs
    chip = lax.div(lax.axis_index("con"), owners)
    step = jnp.bitwise_xor(chip, lax.axis_index("cone"))
    for d, in_ref in enumerate(in_refs):

        @pl.when(step == d)
        def _():
            out_ref[...] = in_ref[...]


def rows_kernel(inverse_ref, panel_ref, *refs):
    *lead_refs, factor_ref, row_ref, lead = refs
    owners = len(lead_refs)
    width = lead_refs[0].shape[1]
    core = lax.rem(lax.axis_index("con"), owners)
    for s, lead_ref in enumerate(lead_refs):
        where = pl.ds(pl.multiple_of(lax.rem(core + s, owners) * width, width), width)
        for g in range(panel_ref.shape[0] // TILE):
            lead[g * TILE : (g + 1) * TILE, where] = decode(lead_ref, g * (TILE + SUB), TILE)
    inverse = split(inverse_ref[...])
    factor_ref[...] = product(inverse, split(panel_ref[...]), PLAIN)
    row_ref[...] = product(inverse, split(lead[...]), PLAIN)


def update_kernel(owners, width, factor_ref, row_ref, own_ref, *refs):
    *code_refs, out_ref = refs
    share = own_ref.shape[0]
    cone = lax.axis_index("cone")
    pivots = lax.axis_index("con") < owners

    @pl.when(cone == 0)
    def _():
        out_ref[...] = factor_ref[...]

    @pl.when(cone != 0)
    def _():
        out_ref[pl.ds(pl.multiple_of(cone * share, share), share), :] = own_ref[...]
        for u, code_ref in enumerate(code_refs, 1):
            other = jnp.bitwise_xor(cone, u) * share
            out_ref[pl.ds(pl.multiple_of(other, share), share), :] = decode(code_ref, 0, share)
        change = product(split(row_ref[...]), split(factor_ref[...]), COLS_T)
        columns = lax.broadcasted_iota(jnp.int32, out_ref.shape, 1)
        out_ref[...] = jnp.where((columns < width) & pivots, 0.0, out_ref[...] - change)


def call(kernel, out_shape, operands, scratch=(), limit=16, scalars=0):
    return pl.pallas_call(
        kernel,
        out_shape=out_shape,
        in_specs=[in_smem()] * scalars + in_vmem(len(operands) - scalars),
        out_specs=jax.tree.map(lambda _: pl.BlockSpec(memory_space=pltpu.VMEM), out_shape),
        scratch_shapes=scratch,
        compiler_params=pltpu.CompilerParams(vmem_limit_bytes=limit << 20),
    )(*operands)


def gather_plan(chips):
    near = ("near", "own", [(z, z ^ 1) for z in range(chips)])
    if chips == 4:
        return [
            near,
            ("middle", "own", [(1, 2), (2, 1)]),
            ("far", "own", [(0, 3), (3, 0)]),
            ("pass_near", "near", [(1, 2), (2, 1)]),
            ("pass_middle", "middle", [(1, 0), (2, 3)]),
        ]
    plan = [near]
    for phase in range(chips // 2):
        for d in reversed(range(2, chips)):
            sources = sorted({phase, chips - 1 - phase})
            plan.append((f"phase_{phase}_{d}", "own", [(b, b ^ d) for b in sources]))
    return plan


def arrivals(chips):
    held = {"own": {z: z for z in range(chips)}}
    for name, sent, moves in gather_plan(chips):
        held[name] = {target: held[sent][source] for source, target in moves}
    return [
        {held[name][z]: name for name, _, _ in gather_plan(chips) if z in held[name]}
        for z in range(chips)
    ]


def block_order(chip, chips):
    names = [name for name, _, _ in gather_plan(chips)]
    by = arrivals(chips)[chip]
    rest = [b for b in range(chips) if b not in (chip, chip ^ 1)]
    return [chip, chip ^ 1] + sorted(rest, key=lambda b: (b != 0, names.index(by[b])))


def shards(vectors, primal, dual_inverse, touches):
    con_count = lax.axis_size("con")
    cones = lax.axis_size("cone")
    per_block, order_n = vectors.shape[1:]
    row_dev = PANEL * cones // con_count
    owners = con_count // cones
    share = PANEL // cones
    steps = min(cones, 3)
    columns, primal_block, dual_block = vectors[0], primal[0], dual_inverse[0]
    order = [block_order(z, cones) for z in range(cones)]

    def exchange(codes, pairs=lambda u: [(i, i ^ u) for i in range(cones)]):
        return [lax.ppermute(code, "cone", pairs(u)) for u, code in enumerate(codes, 1)]

    def along(value, moves):
        pairs = [(a * owners + i, b * owners + i) for a, b in moves for i in range(owners)]
        return lax.ppermute(value, "con", pairs)

    def beside(value):
        swaps = [value]
        for s in range(1, owners):
            pairs = [
                (g * owners + i, g * owners + (i - s) % owners)
                for g in range(cones)
                for i in range(owners)
            ]
            swaps.append(lax.ppermute(value, "con", pairs))
        return swaps

    in_hbm = pl.BlockSpec(memory_space=pltpu.MemorySpace.HBM)
    own_rows = pl.pallas_call(
        mask_kernel,
        out_shape=shaped(row_dev, order_n, BF16),
        in_specs=[in_hbm, in_hbm],
        out_specs=pl.BlockSpec(memory_space=pltpu.VMEM),
        scratch_shapes=[
            pltpu.SMEM(touches.shape, jnp.int32),
            pltpu.SemaphoreType.DMA((2,)),
        ],
        compiler_params=pltpu.CompilerParams(vmem_limit_bytes=2 << 20),
        cost_estimate=pl.CostEstimate(flops=10**10, transcendentals=0, bytes_accessed=10**6),
        name="mask_rows",
    )(touches, pltpu.with_memory_space_constraint(columns, pltpu.MemorySpace.HBM))
    parts = [beside(own_rows)]
    arrived = {"own": own_rows}
    for name, sent, moves in gather_plan(cones):
        arrived[name] = along(arrived[sent], moves)

    for step in range(1, cones):
        wanted = {}
        for z in range(cones):
            wanted.setdefault(arrivals(cones)[z][order[z][step]], []).append(z)
        keys = sorted(wanted)
        mine = call(
            functools.partial(pick_kernel, owners, [wanted[key] for key in keys]),
            shaped(row_dev, order_n, BF16),
            tuple(arrived[key] for key in keys),
            limit=4,
        )
        parts.append(beside(mine))

    coded_square = (PANEL // TILE) * (TILE + SUB)
    terms_shape = (shaped(share, per_block, F32),) + (shaped(share + SUB, per_block, I16),) * (
        cones - 1
    )
    lead_shape = (shaped(PANEL, row_dev, F32), shaped(coded_square, row_dev, I16))
    summed = []
    for step in range(cones):
        first, *codes = call(
            functools.partial(terms_kernel, owners, cones),
            terms_shape + (lead_shape if step == 0 else ()),
            (touches, *parts[step], primal_block, dual_block, columns),
            [
                pltpu.VMEM((PANEL, order_n), BF16),
                pltpu.VMEM((PANEL, per_block), F32),
                pltpu.VMEM((PANEL, order_n), BF16),
                pltpu.VMEM((PANEL, order_n), BF16),
            ],
            18,
            1,
        )
        if step == 0:
            half_own, half_code = codes[cones - 1 :]
        summed.append([first] + exchange(codes[: cones - 1]))

    grid = ("cone", "con")
    half_codes = [
        lax.ppermute(
            half_code,
            grid,
            [(c * con_count + i, (c ^ u) * con_count + i) for c in range(cones) for i in range(owners)],
        )
        for u in range(1, cones)
    ]
    half = call(
        sum_half_kernel, shaped(coded_square, row_dev, I16), (half_own, *half_codes), limit=4
    )
    halves = [half] + [along(half, [(0, d)]) for d in range(1, cones)]
    half = call(
        functools.partial(pick_kernel, owners, [[d] for d in range(cones)]),
        shaped(coded_square, row_dev, I16),
        tuple(halves),
        limit=4,
    )
    work, inverse = call(
        square_kernel,
        (shaped(PANEL, PANEL, F32),) * 2,
        tuple(beside(half)),
        [pltpu.VMEM((PANEL, PANEL), F32)],
        6,
    )
    tiles = PANEL // TILE
    work, inverse = eliminate(work, inverse, 0, tiles // 2)
    work, inverse = eliminate(work, inverse, tiles // 2, tiles)

    panel_own, panel_code = call(
        functools.partial(sum_panel_kernel, owners, cones, steps),
        (shaped(share, per_block, F32), shaped(share + SUB, per_block, I16)),
        tuple(part for group in summed[:steps] for part in group),
        limit=8,
    )
    panel, lead = call(
        gather_panel_kernel,
        (shaped(PANEL, per_block, F32), shaped(coded_square, row_dev, I16)),
        (panel_own, *exchange([panel_code] * (cones - 1))),
        limit=6,
    )
    leads = [lead]
    for d in range(1, cones):
        pairs = [
            (c * con_count + c * owners + i, c * con_count + (c ^ d) * owners + i)
            for c in range(1, cones)
            for i in range(owners)
        ]
        leads.append(lax.ppermute(lead, ("cone", "con"), pairs))
    lead = call(
        functools.partial(pick_lead_kernel, owners),
        shaped(coded_square, row_dev, I16),
        tuple(leads),
        limit=4,
    )
    rest_own, *rest_codes = call(
        functools.partial(sum_rest_kernel, owners, cones),
        terms_shape,
        (jnp.array(order, jnp.int32), *[part for group in summed for part in group]),
        [pltpu.VMEM((cones, share, per_block), F32)],
        16,
        1,
    )
    rest_codes = exchange(rest_codes, lambda u: [(i, i ^ u) for i in range(cones) if i ^ u])
    factor_rows, row_factor = call(
        rows_kernel,
        (shaped(PANEL, per_block, F32), shaped(PANEL, PANEL, F32)),
        (inverse, panel, *beside(lead)),
        [pltpu.VMEM((PANEL, PANEL), F32)],
        14,
    )
    return call(
        functools.partial(update_kernel, owners, row_dev),
        shaped(PANEL, per_block, F32),
        (factor_rows, row_factor, rest_own, *rest_codes),
        limit=14,
    )


def solution(mesh):
    in_specs = (
        P("cone", "con", None),
        P("cone", None, None),
        P("cone", None, None),
        P("cone", None),
    )
    out_specs = P("cone", "con")

    return jax.shard_map(shards, mesh=mesh, in_specs=in_specs, out_specs=out_specs, check_vma=False)
```

```python
import functools
import math

import jax
import jax.numpy as jnp
from jax import lax
from jax.experimental import pallas as pl
from jax.experimental.pallas import tpu as pltpu
from jax.sharding import PartitionSpec as P


PANEL = 512
TILE = 128
SUB = 8
STEPS = 128
LEVELS = 32767.0
OCTAVE = math.log(2.0) / STEPS
ROWS_T = (((1,), (1,)), ((), ()))
COLS_T = (((0,), (0,)), ((), ()))
PLAIN = (((1,), (0,)), ((), ()))
F32 = jnp.float32
BF16 = jnp.bfloat16
I16 = jnp.int16


def in_vmem(count):
    return [pl.BlockSpec(memory_space=pltpu.VMEM)] * count


def in_smem():
    return pl.BlockSpec(memory_space=pltpu.SMEM)


def shaped(rows, columns, dtype):
    return jax.ShapeDtypeStruct((rows, columns), dtype)


def encode(value, out_ref, start):
    rows = value.shape[0]
    top = jnp.max(jnp.abs(value), axis=0, keepdims=True)
    level = jnp.ceil(jnp.log(jnp.maximum(top, 1e-37)) * (1.0 / OCTAVE))
    scaled = value * jnp.exp(level * -OCTAVE) * LEVELS
    whole = jnp.round(jnp.clip(scaled, -LEVELS, LEVELS)).astype(jnp.int32)
    out_ref[start : start + rows, :] = whole.astype(I16)
    levels = jnp.broadcast_to(level, (SUB, value.shape[1])).astype(jnp.int32)
    out_ref[start + rows : start + rows + SUB, :] = levels.astype(I16)


def decode(ref, start, rows):
    whole = ref[start : start + rows, :].astype(jnp.int32).astype(F32)
    level = ref[start + rows : start + rows + SUB, :].astype(jnp.int32).astype(F32)[0:1]
    return whole * (jnp.exp(level * OCTAVE) * (1.0 / LEVELS))


def factor_tile(a):
    groups = TILE // SUB
    rows = lax.broadcasted_iota(jnp.int32, (SUB, TILE), 0)
    lanes = lax.broadcasted_iota(jnp.int32, (SUB, TILE), 1)
    left = [a[g * SUB : (g + 1) * SUB, :] for g in range(groups)]
    right = [jnp.where(lanes == rows + g * SUB, 1.0, 0.0).astype(F32) for g in range(groups)]
    spread = lambda x, j: jnp.broadcast_to(x[:, j : j + 1], (SUB, TILE))
    flat = lambda x, i: jnp.broadcast_to(x[i : i + 1, :], (SUB, TILE))
    first = [spread(x, 0) for x in left]
    second = [spread(x, 1) for x in left]
    scales = [None] * groups
    for j in range(0, TILE, 2):
        g0, i0 = divmod(j, SUB)
        corner, side, end = flat(first[g0], i0), flat(first[g0], i0 + 1), flat(second[g0], i0 + 1)
        by_first = 1.0 / corner
        by_second = corner * (1.0 / (corner * end - side * side))
        slope = side * by_first
        scale = jnp.where(rows == i0, by_first, by_second)
        scales[g0] = scale if i0 == 0 else jnp.where(rows >= i0, scale, scales[g0])
        left_0, right_0 = flat(left[g0], i0), flat(right[g0], i0)
        left_1 = flat(left[g0], i0 + 1) - slope * left_0
        right_1 = flat(right[g0], i0 + 1) - slope * right_0
        more = j + 2 < TILE
        if more:
            g1, i1 = divmod(j + 2, SUB)
            ahead_0 = [spread(left[g], j + 2) if g >= g1 else None for g in range(groups)]
            ahead_1 = [spread(left[g], j + 3) if g >= g1 else None for g in range(groups)]
            p0, q0 = flat(first[g1], i1), flat(first[g1], i1 + 1)
            p1 = flat(second[g1], i1) - slope * p0
            q1 = flat(second[g1], i1 + 1) - slope * q0
        following = [None] * groups, [None] * groups
        for g in range(g0, groups):
            ratio_0 = first[g] * by_first
            ratio_1 = (second[g] - first[g] * slope) * by_second
            if g == g0:
                ratio_0 = jnp.where(rows > i0, ratio_0, 0.0)
                ratio_1 = jnp.where(rows > i0 + 1, ratio_1, 0.0)
            if more and g >= g1:
                following[0][g] = (ahead_0[g] - ratio_0 * p0) - ratio_1 * p1
                following[1][g] = (ahead_1[g] - ratio_0 * q0) - ratio_1 * q1
            left[g] = (left[g] - ratio_0 * left_0) - ratio_1 * left_1
            right[g] = (right[g] - ratio_0 * right_0) - ratio_1 * right_1
        first, second = following
    return jnp.concatenate([r * jnp.sqrt(p) for r, p in zip(right, scales)], axis=0)


def eliminate_kernel(first, last, work_in, x_in, work, x_ref):
    del work_in, x_in
    tiles = work.shape[0] // TILE

    def step(p, carry):
        here = pl.ds(pl.multiple_of(p * TILE, TILE), TILE)
        tile = split(factor_tile(work[here, here]))
        upper = split(product(tile, split(work[here, :]), PLAIN))
        solved = product(tile, split(x_ref[here, :]), PLAIN)
        x_ref[here, :] = solved
        solved = split(solved)
        for q in range(first + 1, tiles):

            @pl.when(q > p)
            def _():
                below = slice(q * TILE, (q + 1) * TILE)
                part = upper[0][:, below], upper[1][:, below]
                work[below, :] -= product(part, upper, COLS_T)
                x_ref[below, :] -= product(part, solved, COLS_T)

        return carry

    lax.fori_loop(first, last, step, 0)


def eliminate(work, x, first, last):
    size = work.shape[0]
    return pl.pallas_call(
        functools.partial(eliminate_kernel, first, last),
        out_shape=(shaped(size, size, F32),) * 2,
        in_specs=in_vmem(2),
        out_specs=tuple(in_vmem(2)),
        input_output_aliases={0: 0, 1: 1},
        compiler_params=pltpu.CompilerParams(vmem_limit_bytes=6 << 20),
    )(work, x)


def square_kernel(*refs):
    *half_refs, work, x_ref, square = refs
    size = x_ref.shape[0]
    owners = len(half_refs)
    width = size // owners
    core = lax.rem(lax.axis_index("con"), owners)
    for s, half_ref in enumerate(half_refs):
        where = lax.rem(core + s, owners) * width
        at = pl.ds(pl.multiple_of(where, TILE), width)
        for g in range(size // TILE):
            square[g * TILE : (g + 1) * TILE, at] = decode(half_ref, g * (TILE + SUB), TILE)
    rows = lax.broadcasted_iota(jnp.int32, (size, size), 0)
    columns = lax.broadcasted_iota(jnp.int32, (size, size), 1)
    value = square[...]
    value = (value + value.T) * 0.5
    diagonal = jnp.where(rows == columns, value, 0.0)
    across = lax.rsqrt(jnp.sum(diagonal, axis=0, keepdims=True))
    down = lax.rsqrt(jnp.sum(diagonal, axis=1, keepdims=True))
    work[...] = value * across * down
    x_ref[...] = jnp.where(rows == columns, across, 0.0)


def weigh(rows_ref, primal_ref, dual_ref, by_primal, by_dual):
    for source, target in ((primal_ref, by_primal), (dual_ref, by_dual)):
        value = jnp.dot(rows_ref[...], source[...], preferred_element_type=F32)
        target[...] = value.astype(BF16)


def hadamard(by_primal, by_dual, columns):
    return lax.dot_general(
        by_primal, columns, ROWS_T, preferred_element_type=F32
    ) * lax.dot_general(by_dual, columns, ROWS_T, preferred_element_type=F32)


def split(value):
    high = value.astype(BF16)
    return high, (value - high.astype(F32)).astype(BF16)


def product(left, right, contract):
    dot = functools.partial(
        lax.dot_general, dimension_numbers=contract, preferred_element_type=F32
    )
    left_high, left_low = left
    right_high, right_low = right
    return dot(left_high, right_high) + (dot(left_high, right_low) + dot(left_low, right_high))


def mask_kernel(touches_ref, rows_ref, out_ref, flags, arrived):
    count = out_ref.shape[0]
    copies = [
        pltpu.make_async_copy(touches_ref, flags, arrived.at[0]),
        pltpu.make_async_copy(rows_ref.at[pl.ds(0, count), :], out_ref, arrived.at[1]),
    ]
    for copy in copies:
        copy.start()
    for copy in copies:
        copy.wait()
    out_ref[...] = out_ref[...] * flags[0, lax.axis_index("con")].astype(BF16)


def pick_kernel(owners, chips, *refs):
    *in_refs, out_ref = refs
    chip = lax.div(lax.axis_index("con"), owners)
    for in_ref, members in zip(in_refs, chips):
        for member in members:

            @pl.when(chip == member)
            def _():
                out_ref[...] = in_ref[...]


def assemble(part_refs, rows):
    owners = len(part_refs)
    count = part_refs[0].shape[0]
    core = lax.rem(lax.axis_index("con"), owners)
    for s, part_ref in enumerate(part_refs):
        where = pl.multiple_of(lax.rem(core + s, owners) * count, count)
        rows[pl.ds(where, count), :] = part_ref[...]


def panel_step(chip):
    return jnp.minimum(chip, 2)


def terms_kernel(owners, cones, touches_ref, *refs):
    part_refs = refs[:owners]
    primal_ref, dual_ref, columns_ref, own_ref = refs[owners : owners + 4]
    code_refs = refs[owners + 4 : owners + 3 + cones]
    lead_refs = refs[owners + 3 + cones : -4]
    rows, value_ref, p_ref, d_ref = refs[-4:]
    assemble(part_refs, rows)
    weigh(rows, primal_ref, dual_ref, p_ref, d_ref)
    flag = touches_ref[0, lax.axis_index("con")].astype(F32)
    value_ref[...] = hadamard(p_ref[...], d_ref[...], columns_ref[...]) * flag
    share = own_ref.shape[0]
    cone = lax.axis_index("cone")
    own_ref[...] = value_ref[pl.ds(pl.multiple_of(cone * share, share), share), :]
    for u, code_ref in enumerate(code_refs, 1):
        other = jnp.bitwise_xor(cone, u) * share
        encode(value_ref[pl.ds(pl.multiple_of(other, share), share), :], code_ref, 0)
    if lead_refs:
        lead_ref, lead_code_ref = lead_refs
        value = value_ref[:, : lead_ref.shape[1]]
        lead_ref[...] = value
        encode_square(value, lead_code_ref)


def encode_square(value, code_ref):
    for g in range(value.shape[0] // TILE):
        encode(value[g * TILE : (g + 1) * TILE], code_ref, g * (TILE + SUB))


def sum_half_kernel(own_ref, *refs):
    *code_refs, out_ref = refs
    for g in range(own_ref.shape[0] // TILE):
        total = own_ref[g * TILE : (g + 1) * TILE, :]
        for code_ref in code_refs:
            total = total + decode(code_ref, g * (TILE + SUB), TILE)
        encode(total, out_ref, g * (TILE + SUB))


def total_of(parts):
    own_ref, *code_refs = parts
    total = own_ref[...]
    for code_ref in code_refs:
        total = total + decode(code_ref, 0, total.shape[0])
    return total


def sum_panel_kernel(owners, cones, steps, *refs):
    sum_ref, out_ref = refs[-2:]
    step = panel_step(lax.div(lax.axis_index("con"), owners))
    for s in range(steps):

        @pl.when(step == s)
        def _():
            total = total_of(refs[s * cones : (s + 1) * cones])
            sum_ref[...] = total
            encode(total, out_ref, 0)


def sum_rest_kernel(owners, cones, order_ref, *refs):
    cone = lax.axis_index("cone")
    chip = lax.div(lax.axis_index("con"), owners)
    inputs = refs[: cones * cones]
    own_ref, *code_refs = refs[cones * cones : cones * cones + cones]
    sums = refs[-1]
    for s in range(cones):
        block = order_ref[chip, s]

        @pl.when(block != 0)
        def _():
            sums[block] = total_of(inputs[s * cones : (s + 1) * cones])

    @pl.when(cone != 0)
    def _():
        own_ref[...] = sums[cone]

    for u, code_ref in enumerate(code_refs, 1):
        other = jnp.bitwise_xor(cone, u)

        @pl.when(other != 0)
        def _():
            encode(sums[other], code_ref, 0)


def gather_panel_kernel(own_ref, *refs):
    *code_refs, panel_ref, lead_ref = refs
    share = own_ref.shape[0]
    cone = lax.axis_index("cone")
    panel_ref[pl.ds(pl.multiple_of(cone * share, share), share), :] = own_ref[...]
    for u, code_ref in enumerate(code_refs, 1):
        other = jnp.bitwise_xor(cone, u) * share
        panel_ref[pl.ds(pl.multiple_of(other, share), share), :] = decode(code_ref, 0, share)
    width = lead_ref.shape[1]
    encode_square(panel_ref[:, :width], lead_ref)


def pick_lead_kernel(owners, *refs):
    *in_refs, out_ref = refs
    chip = lax.div(lax.axis_index("con"), owners)
    step = jnp.bitwise_xor(chip, lax.axis_index("cone"))
    for d, in_ref in enumerate(in_refs):

        @pl.when(step == d)
        def _():
            out_ref[...] = in_ref[...]


def rows_kernel(inverse_ref, panel_ref, *refs):
    *lead_refs, factor_ref, row_ref, lead = refs
    owners = len(lead_refs)
    width = lead_refs[0].shape[1]
    core = lax.rem(lax.axis_index("con"), owners)
    for s, lead_ref in enumerate(lead_refs):
        where = pl.ds(pl.multiple_of(lax.rem(core + s, owners) * width, width), width)
        for g in range(panel_ref.shape[0] // TILE):
            lead[g * TILE : (g + 1) * TILE, where] = decode(lead_ref, g * (TILE + SUB), TILE)
    inverse = split(inverse_ref[...])
    factor_ref[...] = product(inverse, split(panel_ref[...]), PLAIN)
    row_ref[...] = product(inverse, split(lead[...]), PLAIN)


def update_kernel(owners, width, factor_ref, row_ref, own_ref, *refs):
    *code_refs, out_ref = refs
    share = own_ref.shape[0]
    cone = lax.axis_index("cone")
    pivots = lax.axis_index("con") < owners

    @pl.when(cone == 0)
    def _():
        out_ref[...] = factor_ref[...]

    @pl.when(cone != 0)
    def _():
        out_ref[pl.ds(pl.multiple_of(cone * share, share), share), :] = own_ref[...]
        for u, code_ref in enumerate(code_refs, 1):
            other = jnp.bitwise_xor(cone, u) * share
            out_ref[pl.ds(pl.multiple_of(other, share), share), :] = decode(code_ref, 0, share)
        change = product(split(row_ref[...]), split(factor_ref[...]), COLS_T)
        columns = lax.broadcasted_iota(jnp.int32, out_ref.shape, 1)
        out_ref[...] = jnp.where((columns < width) & pivots, 0.0, out_ref[...] - change)


def call(kernel, out_shape, operands, scratch=(), limit=16, scalars=0):
    return pl.pallas_call(
        kernel,
        out_shape=out_shape,
        in_specs=[in_smem()] * scalars + in_vmem(len(operands) - scalars),
        out_specs=jax.tree.map(lambda _: pl.BlockSpec(memory_space=pltpu.VMEM), out_shape),
        scratch_shapes=scratch,
        compiler_params=pltpu.CompilerParams(vmem_limit_bytes=limit << 20),
    )(*operands)


def gather_plan(chips):
    near = ("near", "own", [(z, z ^ 1) for z in range(chips)])
    if chips == 4:
        return [
            near,
            ("middle", "own", [(1, 2), (2, 1)]),
            ("far", "own", [(0, 3), (3, 0)]),
            ("pass_near", "near", [(1, 2), (2, 1)]),
            ("pass_middle", "middle", [(1, 0), (2, 3)]),
        ]
    plan = [near]
    for phase in range(chips // 2):
        for d in reversed(range(2, chips)):
            sources = sorted({phase, chips - 1 - phase})
            plan.append((f"phase_{phase}_{d}", "own", [(b, b ^ d) for b in sources]))
    return plan


def arrivals(chips):
    held = {"own": {z: z for z in range(chips)}}
    for name, sent, moves in gather_plan(chips):
        held[name] = {target: held[sent][source] for source, target in moves}
    return [
        {held[name][z]: name for name, _, _ in gather_plan(chips) if z in held[name]}
        for z in range(chips)
    ]


def block_order(chip, chips):
    names = [name for name, _, _ in gather_plan(chips)]
    by = arrivals(chips)[chip]
    rest = [b for b in range(chips) if b not in (chip, chip ^ 1)]
    return [chip, chip ^ 1] + sorted(rest, key=lambda b: (b != 0, names.index(by[b])))


def shards(vectors, primal, dual_inverse, touches):
    con_count = lax.axis_size("con")
    cones = lax.axis_size("cone")
    per_block, order_n = vectors.shape[1:]
    row_dev = PANEL * cones // con_count
    owners = con_count // cones
    share = PANEL // cones
    steps = min(cones, 3)
    columns, primal_block, dual_block = vectors[0], primal[0], dual_inverse[0]
    order = [block_order(z, cones) for z in range(cones)]

    def exchange(codes):
        return [
            lax.ppermute(code, "cone", [(i, i ^ u) for i in range(cones)])
            for u, code in enumerate(codes, 1)
        ]

    def along(value, moves):
        pairs = [(a * owners + i, b * owners + i) for a, b in moves for i in range(owners)]
        return lax.ppermute(value, "con", pairs)

    def beside(value):
        swaps = [value]
        for s in range(1, owners):
            pairs = [
                (g * owners + i, g * owners + (i - s) % owners)
                for g in range(cones)
                for i in range(owners)
            ]
            swaps.append(lax.ppermute(value, "con", pairs))
        return swaps

    in_hbm = pl.BlockSpec(memory_space=pltpu.MemorySpace.HBM)
    own_rows = pl.pallas_call(
        mask_kernel,
        out_shape=shaped(row_dev, order_n, BF16),
        in_specs=[in_hbm, in_hbm],
        out_specs=pl.BlockSpec(memory_space=pltpu.VMEM),
        scratch_shapes=[
            pltpu.SMEM(touches.shape, jnp.int32),
            pltpu.SemaphoreType.DMA((2,)),
        ],
        compiler_params=pltpu.CompilerParams(vmem_limit_bytes=2 << 20),
        cost_estimate=pl.CostEstimate(flops=10**10, transcendentals=0, bytes_accessed=10**6),
        name="mask_rows",
    )(touches, pltpu.with_memory_space_constraint(columns, pltpu.MemorySpace.HBM))
    parts = [beside(own_rows)]
    arrived = {"own": own_rows}
    for name, sent, moves in gather_plan(cones):
        arrived[name] = along(arrived[sent], moves)

    for step in range(1, cones):
        wanted = {}
        for z in range(cones):
            wanted.setdefault(arrivals(cones)[z][order[z][step]], []).append(z)
        keys = sorted(wanted)
        mine = call(
            functools.partial(pick_kernel, owners, [wanted[key] for key in keys]),
            shaped(row_dev, order_n, BF16),
            tuple(arrived[key] for key in keys),
            limit=4,
        )
        parts.append(beside(mine))

    coded_square = (PANEL // TILE) * (TILE + SUB)
    terms_shape = (shaped(share, per_block, F32),) + (shaped(share + SUB, per_block, I16),) * (
        cones - 1
    )
    lead_shape = (shaped(PANEL, row_dev, F32), shaped(coded_square, row_dev, I16))
    summed = []
    for step in range(cones):
        first, *codes = call(
            functools.partial(terms_kernel, owners, cones),
            terms_shape + (lead_shape if step == 0 else ()),
            (touches, *parts[step], primal_block, dual_block, columns),
            [
                pltpu.VMEM((PANEL, order_n), BF16),
                pltpu.VMEM((PANEL, per_block), F32),
                pltpu.VMEM((PANEL, order_n), BF16),
                pltpu.VMEM((PANEL, order_n), BF16),
            ],
            18,
            1,
        )
        if step == 0:
            half_own, half_code = codes[cones - 1 :]
        summed.append([first] + exchange(codes[: cones - 1]))

    half_codes = exchange([half_code] * (cones - 1))
    half = call(
        sum_half_kernel, shaped(coded_square, row_dev, I16), (half_own, *half_codes), limit=4
    )
    halves = [half] + [along(half, [(0, d)]) for d in range(1, cones)]
    half = call(
        functools.partial(pick_kernel, owners, [[d] for d in range(cones)]),
        shaped(coded_square, row_dev, I16),
        tuple(halves),
        limit=4,
    )
    work, inverse = call(
        square_kernel,
        (shaped(PANEL, PANEL, F32),) * 2,
        tuple(beside(half)),
        [pltpu.VMEM((PANEL, PANEL), F32)],
        6,
    )
    tiles = PANEL // TILE
    work, inverse = eliminate(work, inverse, 0, tiles // 2)
    work, inverse = eliminate(work, inverse, tiles // 2, tiles)

    panel_own, panel_code = call(
        functools.partial(sum_panel_kernel, owners, cones, steps),
        (shaped(share, per_block, F32), shaped(share + SUB, per_block, I16)),
        tuple(part for group in summed[:steps] for part in group),
        limit=8,
    )
    panel, lead = call(
        gather_panel_kernel,
        (shaped(PANEL, per_block, F32), shaped(coded_square, row_dev, I16)),
        (panel_own, *exchange([panel_code] * (cones - 1))),
        limit=6,
    )
    leads = [lead]
    for d in range(1, cones):
        pairs = [
            (c * con_count + c * owners + i, c * con_count + (c ^ d) * owners + i)
            for c in range(1, cones)
            for i in range(owners)
        ]
        leads.append(lax.ppermute(lead, ("cone", "con"), pairs))
    lead = call(
        functools.partial(pick_lead_kernel, owners),
        shaped(coded_square, row_dev, I16),
        tuple(leads),
        limit=4,
    )
    rest_own, *rest_codes = call(
        functools.partial(sum_rest_kernel, owners, cones),
        terms_shape,
        (jnp.array(order, jnp.int32), *[part for group in summed for part in group]),
        [pltpu.VMEM((cones, share, per_block), F32)],
        16,
        1,
    )
    rest_codes = exchange(rest_codes)
    factor_rows, row_factor = call(
        rows_kernel,
        (shaped(PANEL, per_block, F32), shaped(PANEL, PANEL, F32)),
        (inverse, panel, *beside(lead)),
        [pltpu.VMEM((PANEL, PANEL), F32)],
        14,
    )
    return call(
        functools.partial(update_kernel, owners, row_dev),
        shaped(PANEL, per_block, F32),
        (factor_rows, row_factor, rest_own, *rest_codes),
        limit=14,
    )


def solution(mesh):
    in_specs = (
        P("cone", "con", None),
        P("cone", None, None),
        P("cone", None, None),
        P("cone", None),
    )
    out_specs = P("cone", "con")

    return jax.shard_map(shards, mesh=mesh, in_specs=in_specs, out_specs=out_specs, check_vma=False)
```

```python
import functools
import math

import jax
import jax.numpy as jnp
from jax import lax
from jax.experimental import pallas as pl
from jax.experimental.pallas import tpu as pltpu
from jax.sharding import PartitionSpec as P


PANEL = 512
TILE = 128
SUB = 8
STEPS = 128
LEVELS = 32767.0
OCTAVE = math.log(2.0) / STEPS
ROWS_T = (((1,), (1,)), ((), ()))
COLS_T = (((0,), (0,)), ((), ()))
PLAIN = (((1,), (0,)), ((), ()))
F32 = jnp.float32
BF16 = jnp.bfloat16
I16 = jnp.int16


def in_vmem(count):
    return [pl.BlockSpec(memory_space=pltpu.VMEM)] * count


def in_smem():
    return pl.BlockSpec(memory_space=pltpu.SMEM)


def shaped(rows, columns, dtype):
    return jax.ShapeDtypeStruct((rows, columns), dtype)


def encode(value, out_ref, start):
    rows = value.shape[0]
    top = jnp.max(jnp.abs(value), axis=0, keepdims=True)
    level = jnp.ceil(jnp.log(jnp.maximum(top, 1e-37)) * (1.0 / OCTAVE))
    scaled = value * jnp.exp(level * -OCTAVE) * LEVELS
    whole = jnp.round(jnp.clip(scaled, -LEVELS, LEVELS)).astype(jnp.int32)
    out_ref[start : start + rows, :] = whole.astype(I16)
    levels = jnp.broadcast_to(level, (SUB, value.shape[1])).astype(jnp.int32)
    out_ref[start + rows : start + rows + SUB, :] = levels.astype(I16)


def decode(ref, start, rows):
    whole = ref[start : start + rows, :].astype(jnp.int32).astype(F32)
    level = ref[start + rows : start + rows + SUB, :].astype(jnp.int32).astype(F32)[0:1]
    return whole * (jnp.exp(level * OCTAVE) * (1.0 / LEVELS))


def factor_tile(a):
    groups = TILE // SUB
    rows = lax.broadcasted_iota(jnp.int32, (SUB, TILE), 0)
    lanes = lax.broadcasted_iota(jnp.int32, (SUB, TILE), 1)
    left = [a[g * SUB : (g + 1) * SUB, :] for g in range(groups)]
    right = [jnp.where(lanes == rows + g * SUB, 1.0, 0.0).astype(F32) for g in range(groups)]
    spread = lambda x, j: jnp.broadcast_to(x[:, j : j + 1], (SUB, TILE))
    flat = lambda x, i: jnp.broadcast_to(x[i : i + 1, :], (SUB, TILE))
    first = [spread(x, 0) for x in left]
    second = [spread(x, 1) for x in left]
    scales = [None] * groups
    for j in range(0, TILE, 2):
        g0, i0 = divmod(j, SUB)
        corner, side, end = flat(first[g0], i0), flat(first[g0], i0 + 1), flat(second[g0], i0 + 1)
        by_first = 1.0 / corner
        by_second = corner * (1.0 / (corner * end - side * side))
        slope = side * by_first
        scale = jnp.where(rows == i0, by_first, by_second)
        scales[g0] = scale if i0 == 0 else jnp.where(rows >= i0, scale, scales[g0])
        left_0, right_0 = flat(left[g0], i0), flat(right[g0], i0)
        left_1 = flat(left[g0], i0 + 1) - slope * left_0
        right_1 = flat(right[g0], i0 + 1) - slope * right_0
        more = j + 2 < TILE
        if more:
            g1, i1 = divmod(j + 2, SUB)
            ahead_0 = [spread(left[g], j + 2) if g >= g1 else None for g in range(groups)]
            ahead_1 = [spread(left[g], j + 3) if g >= g1 else None for g in range(groups)]
            p0, q0 = flat(first[g1], i1), flat(first[g1], i1 + 1)
            p1 = flat(second[g1], i1) - slope * p0
            q1 = flat(second[g1], i1 + 1) - slope * q0
        following = [None] * groups, [None] * groups
        for g in range(g0, groups):
            ratio_0 = first[g] * by_first
            ratio_1 = (second[g] - first[g] * slope) * by_second
            if g == g0:
                ratio_0 = jnp.where(rows > i0, ratio_0, 0.0)
                ratio_1 = jnp.where(rows > i0 + 1, ratio_1, 0.0)
            if more and g >= g1:
                following[0][g] = (ahead_0[g] - ratio_0 * p0) - ratio_1 * p1
                following[1][g] = (ahead_1[g] - ratio_0 * q0) - ratio_1 * q1
            left[g] = (left[g] - ratio_0 * left_0) - ratio_1 * left_1
            right[g] = (right[g] - ratio_0 * right_0) - ratio_1 * right_1
        first, second = following
    return jnp.concatenate([r * jnp.sqrt(p) for r, p in zip(right, scales)], axis=0)


def eliminate_kernel(first, last, work_in, x_in, work, x_ref):
    del work_in, x_in
    tiles = work.shape[0] // TILE

    def step(p, carry):
        here = pl.ds(pl.multiple_of(p * TILE, TILE), TILE)
        tile = split(factor_tile(work[here, here]))
        upper = split(product(tile, split(work[here, :]), PLAIN))
        solved = product(tile, split(x_ref[here, :]), PLAIN)
        x_ref[here, :] = solved
        solved = split(solved)
        for q in range(first + 1, tiles):

            @pl.when(q > p)
            def _():
                below = slice(q * TILE, (q + 1) * TILE)
                part = upper[0][:, below], upper[1][:, below]
                work[below, :] -= product(part, upper, COLS_T)
                x_ref[below, :] -= product(part, solved, COLS_T)

        return carry

    lax.fori_loop(first, last, step, 0)


def eliminate(work, x, first, last):
    size = work.shape[0]
    return pl.pallas_call(
        functools.partial(eliminate_kernel, first, last),
        out_shape=(shaped(size, size, F32),) * 2,
        in_specs=in_vmem(2),
        out_specs=tuple(in_vmem(2)),
        input_output_aliases={0: 0, 1: 1},
        compiler_params=pltpu.CompilerParams(vmem_limit_bytes=6 << 20),
    )(work, x)


def square_kernel(*refs):
    *half_refs, work, x_ref, square = refs
    size = x_ref.shape[0]
    owners = len(half_refs)
    width = size // owners
    core = lax.rem(lax.axis_index("con"), owners)
    for s, half_ref in enumerate(half_refs):
        where = lax.rem(core + s, owners) * width
        at = pl.ds(pl.multiple_of(where, TILE), width)
        for g in range(size // TILE):
            square[g * TILE : (g + 1) * TILE, at] = decode(half_ref, g * (TILE + SUB), TILE)
    rows = lax.broadcasted_iota(jnp.int32, (size, size), 0)
    columns = lax.broadcasted_iota(jnp.int32, (size, size), 1)
    value = square[...]
    value = (value + value.T) * 0.5
    diagonal = jnp.where(rows == columns, value, 0.0)
    across = lax.rsqrt(jnp.sum(diagonal, axis=0, keepdims=True))
    down = lax.rsqrt(jnp.sum(diagonal, axis=1, keepdims=True))
    work[...] = value * across * down
    x_ref[...] = jnp.where(rows == columns, across, 0.0)


def weigh(rows_ref, primal_ref, dual_ref, by_primal, by_dual):
    for source, target in ((primal_ref, by_primal), (dual_ref, by_dual)):
        value = jnp.dot(rows_ref[...], source[...], preferred_element_type=F32)
        target[...] = value.astype(BF16)


def hadamard(by_primal, by_dual, columns):
    return lax.dot_general(
        by_primal, columns, ROWS_T, preferred_element_type=F32
    ) * lax.dot_general(by_dual, columns, ROWS_T, preferred_element_type=F32)


def split(value):
    high = value.astype(BF16)
    return high, (value - high.astype(F32)).astype(BF16)


def product(left, right, contract):
    dot = functools.partial(
        lax.dot_general, dimension_numbers=contract, preferred_element_type=F32
    )
    left_high, left_low = left
    right_high, right_low = right
    return dot(left_high, right_high) + (dot(left_high, right_low) + dot(left_low, right_high))


def mask_kernel(touches_ref, rows_ref, out_ref, flags, arrived):
    count = out_ref.shape[0]
    copies = [
        pltpu.make_async_copy(touches_ref, flags, arrived.at[0]),
        pltpu.make_async_copy(rows_ref.at[pl.ds(0, count), :], out_ref, arrived.at[1]),
    ]
    for copy in copies:
        copy.start()
    for copy in copies:
        copy.wait()
    out_ref[...] = out_ref[...] * flags[0, lax.axis_index("con")].astype(BF16)


def pick_kernel(owners, chips, *refs):
    *in_refs, out_ref = refs
    chip = lax.div(lax.axis_index("con"), owners)
    for in_ref, members in zip(in_refs, chips):
        for member in members:

            @pl.when(chip == member)
            def _():
                out_ref[...] = in_ref[...]


def assemble(part_refs, rows):
    owners = len(part_refs)
    count = part_refs[0].shape[0]
    core = lax.rem(lax.axis_index("con"), owners)
    for s, part_ref in enumerate(part_refs):
        where = pl.multiple_of(lax.rem(core + s, owners) * count, count)
        rows[pl.ds(where, count), :] = part_ref[...]


def panel_step(chip):
    return jnp.minimum(chip, 2)


def terms_kernel(owners, cones, touches_ref, *refs):
    part_refs = refs[:owners]
    primal_ref, dual_ref, columns_ref, own_ref = refs[owners : owners + 4]
    code_refs = refs[owners + 4 : owners + 3 + cones]
    lead_refs = refs[owners + 3 + cones : -4]
    rows, value_ref, p_ref, d_ref = refs[-4:]
    assemble(part_refs, rows)
    weigh(rows, primal_ref, dual_ref, p_ref, d_ref)
    flag = touches_ref[0, lax.axis_index("con")].astype(F32)
    value_ref[...] = hadamard(p_ref[...], d_ref[...], columns_ref[...]) * flag
    share = own_ref.shape[0]
    cone = lax.axis_index("cone")
    own_ref[...] = value_ref[pl.ds(pl.multiple_of(cone * share, share), share), :]
    for u, code_ref in enumerate(code_refs, 1):
        other = jnp.bitwise_xor(cone, u) * share
        encode(value_ref[pl.ds(pl.multiple_of(other, share), share), :], code_ref, 0)
    if lead_refs:
        lead_ref, lead_code_ref = lead_refs
        value = value_ref[:, : lead_ref.shape[1]]
        lead_ref[...] = value
        encode_square(value, lead_code_ref)


def encode_square(value, code_ref):
    for g in range(value.shape[0] // TILE):
        encode(value[g * TILE : (g + 1) * TILE], code_ref, g * (TILE + SUB))


def sum_half_kernel(own_ref, *refs):
    *code_refs, out_ref = refs
    for g in range(own_ref.shape[0] // TILE):
        total = own_ref[g * TILE : (g + 1) * TILE, :]
        for code_ref in code_refs:
            total = total + decode(code_ref, g * (TILE + SUB), TILE)
        encode(total, out_ref, g * (TILE + SUB))


def total_of(parts):
    own_ref, *code_refs = parts
    total = own_ref[...]
    for code_ref in code_refs:
        total = total + decode(code_ref, 0, total.shape[0])
    return total


def sum_panel_kernel(owners, cones, steps, *refs):
    sum_ref, out_ref = refs[-2:]
    step = panel_step(lax.div(lax.axis_index("con"), owners))
    for s in range(steps):

        @pl.when(step == s)
        def _():
            total = total_of(refs[s * cones : (s + 1) * cones])
            sum_ref[...] = total
            encode(total, out_ref, 0)


def sum_rest_kernel(owners, cones, order_ref, *refs):
    cone = lax.axis_index("cone")
    chip = lax.div(lax.axis_index("con"), owners)
    inputs = refs[: cones * cones]
    own_ref, *code_refs = refs[cones * cones : cones * cones + cones]
    sums = refs[-1]
    for s in range(cones):
        block = order_ref[chip, s]

        @pl.when(block != 0)
        def _():
            sums[block] = total_of(inputs[s * cones : (s + 1) * cones])

    @pl.when(cone != 0)
    def _():
        own_ref[...] = sums[cone]

    for u, code_ref in enumerate(code_refs, 1):
        other = jnp.bitwise_xor(cone, u)

        @pl.when(other != 0)
        def _():
            encode(sums[other], code_ref, 0)


def gather_panel_kernel(own_ref, *refs):
    *code_refs, panel_ref, lead_ref = refs
    share = own_ref.shape[0]
    cone = lax.axis_index("cone")
    panel_ref[pl.ds(pl.multiple_of(cone * share, share), share), :] = own_ref[...]
    for u, code_ref in enumerate(code_refs, 1):
        other = jnp.bitwise_xor(cone, u) * share
        panel_ref[pl.ds(pl.multiple_of(other, share), share), :] = decode(code_ref, 0, share)
    width = lead_ref.shape[1]
    encode_square(panel_ref[:, :width], lead_ref)


def pick_lead_kernel(owners, *refs):
    *in_refs, out_ref = refs
    chip = lax.div(lax.axis_index("con"), owners)
    step = jnp.bitwise_xor(chip, lax.axis_index("cone"))
    for d, in_ref in enumerate(in_refs):

        @pl.when(step == d)
        def _():
            out_ref[...] = in_ref[...]


def factor_rows_kernel(inverse_ref, panel_ref, factor_ref):
    factor_ref[...] = product(split(inverse_ref[...]), split(panel_ref[...]), PLAIN)


def rows_kernel(inverse_ref, *refs):
    *lead_refs, row_ref, lead = refs
    owners = len(lead_refs)
    width = lead_refs[0].shape[1]
    core = lax.rem(lax.axis_index("con"), owners)
    for s, lead_ref in enumerate(lead_refs):
        where = pl.ds(pl.multiple_of(lax.rem(core + s, owners) * width, width), width)
        for g in range(lead.shape[0] // TILE):
            lead[g * TILE : (g + 1) * TILE, where] = decode(lead_ref, g * (TILE + SUB), TILE)
    row_ref[...] = product(split(inverse_ref[...]), split(lead[...]), PLAIN)


def update_kernel(owners, width, factor_ref, row_ref, own_ref, *refs):
    *code_refs, out_ref = refs
    share = own_ref.shape[0]
    cone = lax.axis_index("cone")
    pivots = lax.axis_index("con") < owners

    @pl.when(cone == 0)
    def _():
        out_ref[...] = factor_ref[...]

    @pl.when(cone != 0)
    def _():
        out_ref[pl.ds(pl.multiple_of(cone * share, share), share), :] = own_ref[...]
        for u, code_ref in enumerate(code_refs, 1):
            other = jnp.bitwise_xor(cone, u) * share
            out_ref[pl.ds(pl.multiple_of(other, share), share), :] = decode(code_ref, 0, share)
        change = product(split(row_ref[...]), split(factor_ref[...]), COLS_T)
        columns = lax.broadcasted_iota(jnp.int32, out_ref.shape, 1)
        out_ref[...] = jnp.where((columns < width) & pivots, 0.0, out_ref[...] - change)


def call(kernel, out_shape, operands, scratch=(), limit=16, scalars=0):
    return pl.pallas_call(
        kernel,
        out_shape=out_shape,
        in_specs=[in_smem()] * scalars + in_vmem(len(operands) - scalars),
        out_specs=jax.tree.map(lambda _: pl.BlockSpec(memory_space=pltpu.VMEM), out_shape),
        scratch_shapes=scratch,
        compiler_params=pltpu.CompilerParams(vmem_limit_bytes=limit << 20),
    )(*operands)


def gather_plan(chips):
    near = ("near", "own", [(z, z ^ 1) for z in range(chips)])
    if chips == 4:
        return [
            near,
            ("middle", "own", [(1, 2), (2, 1)]),
            ("far", "own", [(0, 3), (3, 0)]),
            ("pass_near", "near", [(1, 2), (2, 1)]),
            ("pass_middle", "middle", [(1, 0), (2, 3)]),
        ]
    plan = [near]
    for phase in range(chips // 2):
        for d in reversed(range(2, chips)):
            sources = sorted({phase, chips - 1 - phase})
            plan.append((f"phase_{phase}_{d}", "own", [(b, b ^ d) for b in sources]))
    return plan


def arrivals(chips):
    held = {"own": {z: z for z in range(chips)}}
    for name, sent, moves in gather_plan(chips):
        held[name] = {target: held[sent][source] for source, target in moves}
    return [
        {held[name][z]: name for name, _, _ in gather_plan(chips) if z in held[name]}
        for z in range(chips)
    ]


def block_order(chip, chips):
    names = [name for name, _, _ in gather_plan(chips)]
    by = arrivals(chips)[chip]
    rest = [b for b in range(chips) if b not in (chip, chip ^ 1)]
    return [chip, chip ^ 1] + sorted(rest, key=lambda b: (b != 0, names.index(by[b])))


def shards(vectors, primal, dual_inverse, touches):
    con_count = lax.axis_size("con")
    cones = lax.axis_size("cone")
    per_block, order_n = vectors.shape[1:]
    row_dev = PANEL * cones // con_count
    owners = con_count // cones
    share = PANEL // cones
    steps = min(cones, 3)
    columns, primal_block, dual_block = vectors[0], primal[0], dual_inverse[0]
    order = [block_order(z, cones) for z in range(cones)]

    def exchange(codes):
        return [
            lax.ppermute(code, "cone", [(i, i ^ u) for i in range(cones)])
            for u, code in enumerate(codes, 1)
        ]

    def along(value, moves):
        pairs = [(a * owners + i, b * owners + i) for a, b in moves for i in range(owners)]
        return lax.ppermute(value, "con", pairs)

    def beside(value):
        swaps = [value]
        for s in range(1, owners):
            pairs = [
                (g * owners + i, g * owners + (i - s) % owners)
                for g in range(cones)
                for i in range(owners)
            ]
            swaps.append(lax.ppermute(value, "con", pairs))
        return swaps

    in_hbm = pl.BlockSpec(memory_space=pltpu.MemorySpace.HBM)
    own_rows = pl.pallas_call(
        mask_kernel,
        out_shape=shaped(row_dev, order_n, BF16),
        in_specs=[in_hbm, in_hbm],
        out_specs=pl.BlockSpec(memory_space=pltpu.VMEM),
        scratch_shapes=[
            pltpu.SMEM(touches.shape, jnp.int32),
            pltpu.SemaphoreType.DMA((2,)),
        ],
        compiler_params=pltpu.CompilerParams(vmem_limit_bytes=2 << 20),
        cost_estimate=pl.CostEstimate(flops=10**10, transcendentals=0, bytes_accessed=10**6),
        name="mask_rows",
    )(touches, pltpu.with_memory_space_constraint(columns, pltpu.MemorySpace.HBM))
    parts = [beside(own_rows)]
    arrived = {"own": own_rows}
    for name, sent, moves in gather_plan(cones):
        arrived[name] = along(arrived[sent], moves)

    for step in range(1, cones):
        wanted = {}
        for z in range(cones):
            wanted.setdefault(arrivals(cones)[z][order[z][step]], []).append(z)
        keys = sorted(wanted)
        mine = call(
            functools.partial(pick_kernel, owners, [wanted[key] for key in keys]),
            shaped(row_dev, order_n, BF16),
            tuple(arrived[key] for key in keys),
            limit=4,
        )
        parts.append(beside(mine))

    coded_square = (PANEL // TILE) * (TILE + SUB)
    terms_shape = (shaped(share, per_block, F32),) + (shaped(share + SUB, per_block, I16),) * (
        cones - 1
    )
    lead_shape = (shaped(PANEL, row_dev, F32), shaped(coded_square, row_dev, I16))
    summed = []
    for step in range(cones):
        first, *codes = call(
            functools.partial(terms_kernel, owners, cones),
            terms_shape + (lead_shape if step == 0 else ()),
            (touches, *parts[step], primal_block, dual_block, columns),
            [
                pltpu.VMEM((PANEL, order_n), BF16),
                pltpu.VMEM((PANEL, per_block), F32),
                pltpu.VMEM((PANEL, order_n), BF16),
                pltpu.VMEM((PANEL, order_n), BF16),
            ],
            18,
            1,
        )
        if step == 0:
            half_own, half_code = codes[cones - 1 :]
        summed.append([first] + exchange(codes[: cones - 1]))

    half_codes = exchange([half_code] * (cones - 1))
    half = call(
        sum_half_kernel, shaped(coded_square, row_dev, I16), (half_own, *half_codes), limit=4
    )
    halves = [half] + [along(half, [(0, d)]) for d in range(1, cones)]
    half = call(
        functools.partial(pick_kernel, owners, [[d] for d in range(cones)]),
        shaped(coded_square, row_dev, I16),
        tuple(halves),
        limit=4,
    )
    work, inverse = call(
        square_kernel,
        (shaped(PANEL, PANEL, F32),) * 2,
        tuple(beside(half)),
        [pltpu.VMEM((PANEL, PANEL), F32)],
        6,
    )
    tiles = PANEL // TILE
    work, inverse = eliminate(work, inverse, 0, tiles // 2)
    work, inverse = eliminate(work, inverse, tiles // 2, tiles)

    panel_own, panel_code = call(
        functools.partial(sum_panel_kernel, owners, cones, steps),
        (shaped(share, per_block, F32), shaped(share + SUB, per_block, I16)),
        tuple(part for group in summed[:steps] for part in group),
        limit=8,
    )
    panel, lead = call(
        gather_panel_kernel,
        (shaped(PANEL, per_block, F32), shaped(coded_square, row_dev, I16)),
        (panel_own, *exchange([panel_code] * (cones - 1))),
        limit=6,
    )
    leads = [lead]
    for d in range(1, cones):
        pairs = [
            (c * con_count + c * owners + i, c * con_count + (c ^ d) * owners + i)
            for c in range(1, cones)
            for i in range(owners)
        ]
        leads.append(lax.ppermute(lead, ("cone", "con"), pairs))
    lead = call(
        functools.partial(pick_lead_kernel, owners),
        shaped(coded_square, row_dev, I16),
        tuple(leads),
        limit=4,
    )
    rest_own, *rest_codes = call(
        functools.partial(sum_rest_kernel, owners, cones),
        terms_shape,
        (jnp.array(order, jnp.int32), *[part for group in summed for part in group]),
        [pltpu.VMEM((cones, share, per_block), F32)],
        16,
        1,
    )
    rest_codes = exchange(rest_codes)
    factor_rows = call(
        factor_rows_kernel, shaped(PANEL, per_block, F32), (inverse, panel), limit=12
    )
    row_factor = call(
        rows_kernel,
        shaped(PANEL, PANEL, F32),
        (inverse, *beside(lead)),
        [pltpu.VMEM((PANEL, PANEL), F32)],
        10,
    )
    return call(
        functools.partial(update_kernel, owners, row_dev),
        shaped(PANEL, per_block, F32),
        (factor_rows, row_factor, rest_own, *rest_codes),
        limit=14,
    )


def solution(mesh):
    in_specs = (
        P("cone", "con", None),
        P("cone", None, None),
        P("cone", None, None),
        P("cone", None),
    )
    out_specs = P("cone", "con")

    return jax.shard_map(shards, mesh=mesh, in_specs=in_specs, out_specs=out_specs, check_vma=False)
```
